32 devices in a mesh: wafer: 2 (over x), die: 16 (over z, y, core).
Axes of the slice: x: 2, y: 2, z: 4, core: 2. Of those that a mesh axis runs over, the one named last changes fastest.
Arguments:
- die_tiles: float32 [512, 64, 1024], P(('wafer', 'die')), parts along dimension 0, may hold values from -14 to 14
- slot_pos: int32 [512], P(('wafer', 'die')), parts along dimension 0, may hold values from 0 to 31, as said below
- slot_die: int32 [512], P(('wafer', 'die')), parts along dimension 0, may hold values from 0 to 7
- present: int32 [16, 32], P('wafer'), parts along dimension 0, may hold values from 0 to 1, as said below
- strength: float32 [32, 64, 1024], P('die'), may hold values from 0.3 to 3
- kernel: float32 [5, 5], replicated, may hold values from 0.1 to 1
Outputs:
- residual: float32 [512, 64, 1024], P(('wafer', 'die')), parts along dimension 0
The draws below stay inside these ranges and needn't reach their ends.
There are 2 independent parts, one for each index of `wafer`. The reference program is written for one: setup_inputs(seed, part) draws one part's arguments, and reference() takes and returns one part's arrays. A program takes and returns all parts, laid end to end along the dimension named above; an argument that names none is the same for every part. Nothing has to cross between parts.
Inputs may be any that keep to these rules, and one draw needn't show every extreme that they name: `slot_pos`: each pair of position and die stands in exactly one slot. Among the slots of one device, at most 2 hold positions with equal position // 2, and this most is reached on every device; every value of position // 2 is held by 16 slots in all. At every position at least 6 dies are present.
All inputs are finite; a program needn't handle non-finite values.
Results may differ from the reference program's by a relative error of at most 0.0001.
Values sent between devices are 32-bit elements; how exact they have to be, the bound alone decides.
A program may use at most 128 MiB of HBM per device.

```python
import math
import jax
import jax.numpy as jnp

COLS = 1024
ROWS = 64
POS_DEV = 2
ITERS = 3
SLOTS = 16
TILES = 256
POSITIONS = 32
DIES = 8


def layout(key):
    count = SLOTS
    base = jax.random.fold_in(key, 11)
    first = jax.random.fold_in(base, 1)
    second = jax.random.fold_in(base, 2)
    third = jax.random.fold_in(base, 3)
    sigma = jax.random.permutation(first, count)
    index = jnp.arange(count, dtype=jnp.int32)
    offset = (index[None, :] - sigma[:, None]) % count
    quarter = count // 4
    counts = 1 + (offset < quarter).astype(jnp.int32) - ((offset >= quarter) & (offset < 2 * quarter)).astype(jnp.int32)
    cumul = jnp.cumsum(counts, axis=0)
    dealt = jax.vmap(lambda sub: jax.random.permutation(sub, count))(jax.random.split(second, count))
    source = jnp.sum((cumul.T[:, :, None] <= index[None, None, :]).astype(jnp.int32), axis=1)
    start = (cumul - counts).T
    within = index[None, :] - jnp.take_along_axis(start, source, axis=1)
    before = (jnp.cumsum(counts, axis=1) - counts).T
    source_rank = jnp.take_along_axis(before, source, axis=1) + within
    shuffle = jax.vmap(lambda sub: jax.random.permutation(sub, count))(jax.random.split(third, count))
    local_slot = shuffle[source.ravel(), source_rank.ravel()]
    global_slot = source.ravel() * count + local_slot
    owner = jnp.repeat(index, count)
    tile_id = dealt.ravel()
    position = owner * POS_DEV + tile_id // DIES
    die_id = tile_id % DIES
    slot_position = jnp.zeros((TILES,), jnp.int32).at[global_slot].set(position.astype(jnp.int32))
    slot_dies = jnp.zeros((TILES,), jnp.int32).at[global_slot].set(die_id.astype(jnp.int32))
    return (slot_position, slot_dies)


def draw_slot_pos(key, part):
    return layout(key)[0]


def draw_slot_die(key, part):
    return layout(key)[1]


def draw_present(key, part):
    first = jax.random.fold_in(key, 21)
    second = jax.random.fold_in(key, 22)
    edge = jax.random.permutation(first, DIES) < DIES // 4
    coin = jax.random.randint(second, (DIES, POSITIONS), 0, 2)
    return jnp.where(edge[:, None], coin, 1).astype(jnp.int32)


def draw_die_tiles(key, part):
    slot_position = layout(key)[0]
    pattern = jnp.clip(1.5 * jax.random.normal(jax.random.fold_in(key, 31), (POSITIONS, ROWS, COLS), jnp.float32), -5.0, 5.0)
    noise = jnp.clip(0.5 * jax.random.normal(jax.random.fold_in(key, 32), (TILES, ROWS, COLS), jnp.float32), -2.5, 2.5)
    chance = jax.random.uniform(jax.random.fold_in(key, 33), (TILES, ROWS, COLS), jnp.float32)
    height = jax.random.uniform(jax.random.fold_in(key, 34), (TILES, ROWS, COLS), jnp.float32, 1.5, 4.0)
    flip = jnp.where(jax.random.uniform(jax.random.fold_in(key, 35), (TILES, ROWS, COLS), jnp.float32) < 0.15, -1.0, 1.0)
    defect = jnp.where(chance < 0.3, flip * height, 0.0)
    return (pattern[slot_position] + noise + defect).astype(jnp.float32)


def level_of(rng, dims, cuts, least, high):
    factor_of, own = 1.0, jax.random.fold_in(rng, 6)
    for dim, blocks in cuts:
        heights = jnp.exp(jax.random.uniform(jax.random.fold_in(own, dim), (blocks,), jnp.float32, least / len(cuts), high / len(cuts)))
        factor_of = factor_of * jnp.repeat(heights, dims[dim] // blocks).reshape([-1 if axis == dim else 1 for axis in range(len(dims))])
    return factor_of


def setup_inputs(seed: int = 0, part: int = 0) -> dict:
    keys = jax.random.split(jax.random.key(seed), 7)
    part_keys = jax.random.split(jax.random.fold_in(keys[6], part), 7)
    die_tiles = draw_die_tiles(jax.random.fold_in(jax.random.fold_in(keys[6], part), 71), part)
    slot_pos = draw_slot_pos(jax.random.fold_in(jax.random.fold_in(keys[6], part), 71), part)
    slot_die = draw_slot_die(jax.random.fold_in(jax.random.fold_in(keys[6], part), 71), part)
    present = draw_present(jax.random.fold_in(jax.random.fold_in(keys[6], part), 71), part)
    strength = jnp.clip(jnp.exp(math.log(3.0) - 2.3025851 * jax.random.uniform(keys[4], (POSITIONS, ROWS, COLS), jnp.float32) ** level_of(keys[4], (POSITIONS, ROWS, COLS), ((0, 16),), -0.2, 0.2)), 0.3, 3.0)
    kernel = jnp.clip(jax.random.uniform(keys[5], (5, 5), jnp.float32, 0.1, 1.0), 0.1, 1.0)
    return dict(die_tiles=die_tiles, slot_pos=slot_pos, slot_die=slot_die, present=present, strength=strength, kernel=kernel)


def smooth(field, strength, kernel):
    rows = field.shape[1]
    cols = field.shape[2]
    padded = jnp.pad(field, ((0, 0), (2, 2), (2, 2)))
    total = jnp.zeros_like(field)
    for shift_row in range(5):
        for shift_col in range(5):
            total = total + kernel[shift_row, shift_col] * padded[:, shift_row:shift_row + rows, shift_col:shift_col + cols]
    return (field + strength * total) / (1.0 + strength * jnp.sum(kernel))


def reference(die_tiles, slot_pos, slot_die, present, strength, kernel):
    rows = die_tiles.shape[1]
    cols = die_tiles.shape[2]
    pair = (slot_pos * DIES + slot_die).astype(jnp.int32)
    where_slot = jnp.zeros((TILES,), jnp.int32).at[pair].set(jnp.arange(TILES, dtype=jnp.int32))
    stack = die_tiles[where_slot].reshape(POSITIONS, DIES, rows, cols)
    live = present.T.astype(jnp.float32)
    weight0 = live[:, :, None, None]
    mean = jnp.sum(weight0 * stack, axis=1) / jnp.sum(live, axis=1)[:, None, None]
    refer = mean
    for step in range(ITERS):
        gap = jnp.abs(stack - refer[:, None])
        weight = weight0 * 1.5 / jnp.maximum(gap, 1.5)
        mean = jnp.sum(weight * stack, axis=1) / jnp.sum(weight, axis=1)
        refer = smooth(mean, strength, kernel)
    keep = present[slot_die, slot_pos].astype(jnp.float32)
    return keep[:, None, None] * (die_tiles - refer[slot_pos])
```

```python
import functools

import jax
import jax.numpy as jnp
from jax import lax
from jax.experimental import pallas as pl
from jax.experimental.pallas import tpu as pltpu
from jax.sharding import PartitionSpec as P

ITERS = 3
RS = 8
LANES = 128
PARTS = 4
HALVES = 2
PER_STEP = 2


def strip_of(q, strips):
    odd = q % 2
    half = q // 2
    return half * (1 - odd) + (strips - 1 - half) * odd


def chip_of(s, strips):
    high = s // (strips // 2)
    return 2 * s * (1 - high) + (2 * (strips - 1 - s) + 1) * high


def greet(n):
    me = lax.axis_index("die")
    barrier = pltpu.get_barrier_semaphore()
    for k in range(1, n):
        pl.semaphore_signal(barrier, inc=1, device_id={"die": (me + k) % n}, device_id_type=pl.DeviceIdType.MESH)
    pl.semaphore_wait(barrier, n - 1)


def remote(src, dst, send, recv, device):
    return pltpu.make_async_remote_copy(
        src_ref=src, dst_ref=dst, send_sem=send, recv_sem=recv,
        device_id={"die": device}, device_id_type=pl.DeviceIdType.MESH,
    )


def refer_kernel(
    n, strips, blocks, cs, dies, positions,
    live, kern, pair, tiles, power, out,
    stacks, strength, pairs, table, where, mean,
    top, bottom, rows_up, rows_down, side_left, side_right, corners, ext, refer,
    send, recv, psend, precv, qsend, qrecv, local, hsend, hrecv, rsend, rrecv, ssend, srecv, own,
):
    me = lax.axis_index("die")
    slots = tiles.shape[0]
    held = power.shape[0]
    chunks = cs // LANES
    s = strip_of(me // blocks, strips)
    c = me % blocks
    groups = positions // 4

    def device(ds, dc):
        return chip_of((s + ds + strips) % strips, strips) * blocks + (c + dc + blocks) % blocks

    def rows_of(peer):
        return pl.ds(pl.multiple_of(strip_of(peer // blocks, strips) * RS, RS), RS)

    def cols_of(peer, start, size):
        return pl.ds(pl.multiple_of((peer % blocks) * cs + start, LANES), size)

    tile_rows = pl.ds(me * slots, slots)
    power_rows = pl.ds(me * held, held)
    greet(n)
    pair_copies = [pltpu.make_async_copy(pair, pairs.at[tile_rows], local.at[0])]
    for k in range(1, n):
        pair_copies.append(remote(pair, pairs.at[tile_rows], qsend.at[k], qrecv.at[k], (me + k) % n))
    for copy in pair_copies:
        copy.start()
    tile_copies = []
    for u in range(chunks):
        wave = [
            pltpu.make_async_copy(
                tiles.at[:, rows_of(me), cols_of(me, u * LANES, LANES)], stacks[u].at[tile_rows], local.at[2 + u]
            )
        ]
        for k in range(1, n):
            peer = (me + k) % n
            wave.append(
                remote(
                    tiles.at[:, rows_of(peer), cols_of(peer, u * LANES, LANES)], stacks[u].at[tile_rows],
                    send.at[u, k], recv.at[u, k], peer,
                )
            )
        for copy in wave:
            copy.start()
        tile_copies.append(wave)
    power_copies = [
        pltpu.make_async_copy(power.at[:, rows_of(me), cols_of(me, 0, cs)], strength.at[power_rows], local.at[1])
    ]
    for k in range(1, n):
        peer = (me + k) % n
        power_copies.append(
            remote(
                power.at[:, rows_of(peer), cols_of(peer, 0, cs)], strength.at[power_rows],
                psend.at[k], precv.at[k], peer,
            )
        )
    for copy in power_copies:
        copy.start()

    for copy in pair_copies:
        copy.wait()
    order = lax.broadcasted_iota(jnp.int32, (n * slots, LANES), 0)
    target = lax.broadcasted_iota(jnp.int32, (n * slots, LANES), 1)
    for w in range(table.shape[0]):
        hit = pairs[...] == target + w * LANES
        table[w : w + 1, :] = jnp.max(jnp.where(hit, order, 0), axis=0, keepdims=True)
    fetch = pltpu.make_async_copy(table, where, local.at[2 + chunks])
    fetch.start()
    fetch.wait()

    def value_of(p, d, some):
        q = p * dies + d
        entry = where[q // LANES, q % LANES]
        if len(some) == 1:
            return stacks[some[0]][entry]
        return jnp.concatenate([stacks[u][entry] for u in some], axis=1)

    first = pl.ds(0, LANES)
    last = pl.ds(cs - LANES, LANES)
    taps = [[kern[5 * a + b] for b in range(5)] for a in range(5)]
    total = taps[0][0]
    for a in range(5):
        for b in range(5):
            if a or b:
                total = total + taps[a][b]

    def exchange(k, h):
        size = groups // HALVES
        g = pl.ds(h * size, size)
        p = pl.ds(h * size * 4, size * 4)
        moves = [
            (bottom.at[k, g], rows_up.at[k, g], 1, 0),
            (top.at[k, g], rows_down.at[k, g], -1, 0),
            (mean.at[k, p, :, last], side_left.at[k, p], 0, 1),
            (mean.at[k, p, :, first], side_right.at[k, p], 0, -1),
            (bottom.at[k, g, :, last], corners.at[k, 0, g], 1, 1),
            (bottom.at[k, g, :, first], corners.at[k, 1, g], 1, -1),
            (top.at[k, g, :, last], corners.at[k, 2, g], -1, 1),
            (top.at[k, g, :, first], corners.at[k, 3, g], -1, -1),
        ]
        copies = [
            remote(src, dst, hsend.at[k, h, m], hrecv.at[k, h, m], device(ds, dc))
            for m, (src, dst, ds, dc) in enumerate(moves)
        ]
        for copy in copies:
            copy.start()
        return copies

    def guard(flag, x):
        return jnp.where(flag, x, jnp.zeros_like(x))

    has_up, has_down, has_left, has_right = s > 0, s < strips - 1, c > 0, c < blocks - 1
    body = pl.ds(LANES, cs)
    right = pl.ds(LANES + cs, LANES)

    def smooth(k, g, j):
        p = 4 * g + j
        pair = pl.ds(2 * j, 2)
        field = mean[k, p]
        ext[j, 6:8, first] = guard(has_up & has_left, corners[k, 0, g, pair, :])
        ext[j, 6:8, body] = guard(has_up, rows_up[k, g, pair, :])
        ext[j, 6:8, right] = guard(has_up & has_right, corners[k, 1, g, pair, :])
        ext[j, 8:16, first] = guard(has_left, side_left[k, p])
        ext[j, 8:16, body] = field
        ext[j, 8:16, right] = guard(has_right, side_right[k, p])
        ext[j, 16:18, first] = guard(has_down & has_left, corners[k, 2, g, pair, :])
        ext[j, 16:18, body] = guard(has_down, rows_down[k, g, pair, :])
        ext[j, 16:18, right] = guard(has_down & has_right, corners[k, 3, g, pair, :])
        shifted = [ext[j, 6 + a : 14 + a, :] for a in range(5)]
        width = cs + 2 * LANES
        acc = None
        for b in range(5):
            part = shifted[0] * taps[0][b]
            for a in range(1, 5):
                part = part + shifted[a] * taps[a][b]
            if b != 2:
                part = pltpu.roll(part, (2 - b) % width, 1)
            part = part[:, LANES : LANES + cs]
            acc = part if acc is None else acc + part
        power_p = strength[p]
        return (field + power_p * acc) / (1.0 + power_p * total)

    def huber(k, g, j, ref, some):
        lanes = pl.ds(some[0] * LANES, len(some) * LANES)
        p = 4 * g + j
        num = None
        for d in range(dies):
            value = value_of(p, d, some)
            weight = live[p * dies + d] / jnp.maximum(jnp.abs(value - ref), 1.5)
            num, den = (weight * value, weight) if num is None else (num + weight * value, den + weight)
        field = num / den
        mean[k, p, :, lanes] = field
        top[k, g, 2 * j : 2 * j + 2, lanes] = field[0:2]
        bottom[k, g, 2 * j : 2 * j + 2, lanes] = field[RS - 2 : RS]

    for u in range(chunks):
        some = (u,)
        for copy in tile_copies[u]:
            copy.wait()

        @pl.loop(0, groups)
        def _(g):
            for j in range(4):
                p = 4 * g + j
                count = live[p * dies]
                num = count * value_of(p, 0, some)
                for d in range(1, dies):
                    share = live[p * dies + d]
                    count = count + share
                    num = num + share * value_of(p, d, some)
                huber(0, g, j, num / jnp.full(num.shape, count), some)

    halo = [exchange(0, h) for h in range(HALVES)]
    for copy in power_copies:
        copy.wait()
    for k in range(1, ITERS):
        later = []
        for h in range(HALVES):
            for copy in halo[h]:
                copy.wait()

            @pl.loop(h * groups // HALVES, (h + 1) * groups // HALVES)
            def _(g):
                for j in range(4):
                    huber(k, g, j, smooth(k - 1, g, j), tuple(range(chunks)))

            later.append(exchange(k, h))
        halo = later

    turn = 1 - 2 * (c % 2)
    ahead = device(turn, 0)
    parts = rsend.shape[1]
    span = positions // parts
    pending = []
    rings = {}
    mine = []

    def forward(t, h):
        strip = (s - turn * t + strips) % strips
        part = pl.ds(h * span, span)
        target = out.at[strip, c, part]
        block = target if t else refer.at[part]
        if t:
            rings[t - 1, h].wait_recv()
        copies = [remote(block, target, ssend.at[t, h, b], srecv.at[t, h, b], device(0, b)) for b in range(1, blocks)]
        if t < strips - 1:
            rings[t, h] = remote(block, target, rsend.at[t, h], rrecv.at[t, h], ahead)
            copies.insert(0, rings[t, h])
        for copy in copies:
            copy.start()
        pending.extend(copies)

    for h in range(parts):
        if h * HALVES % parts == 0:
            for copy in halo[h * HALVES // parts]:
                copy.wait()

        @pl.loop(h * span // 4, (h + 1) * span // 4)
        def _(g):
            for j in range(4):
                refer[4 * g + j] = smooth(ITERS - 1, g, j)

        part = pl.ds(h * span, span)
        mine.append(pltpu.make_async_copy(refer.at[part], out.at[s, c, part], own.at[h]))
        mine[-1].start()
        forward(0, h)
    for t in range(1, strips):
        for h in range(parts):
            forward(t, h)
    for copy in pending:
        copy.wait_send()
    for t in range(strips):
        for h in range(parts):
            for b in range(1, blocks):
                source = (c - b + blocks) % blocks
                strip = (s - (1 - 2 * (source % 2)) * t + strips) % strips
                target = out.at[strip, source, pl.ds(h * span, span)]
                remote(target, target, ssend.at[t, h, b], srecv.at[t, h, b], device(0, b)).wait_recv()
    for copy in mine:
        copy.wait()


def residual_kernel(strips, blocks, cs, pos, die, present, tile, *rest):
    out = rest[-1]
    for u in range(PER_STEP):
        slot = pl.program_id(0) * PER_STEP + u
        keep = present[die[slot], pos[slot]].astype(jnp.float32)
        for s in range(strips):
            for c in range(blocks):
                rows, cols = pl.ds(s * RS, RS), pl.ds(c * cs, cs)
                out[u, rows, cols] = keep * (tile[u, rows, cols] - rest[u][s, c, 0])


def refer_spec(strips, blocks, cs, u):
    return pl.BlockSpec((strips, blocks, 1, RS, cs), lambda i, pos, *_: (0, 0, pos[i * PER_STEP + u], 0, 0))


def shards(n, die_tiles, slot_pos, slot_die, present, strength, kernel):
    slots, rows, cols = die_tiles.shape
    dies, positions = present.shape
    strips = rows // RS
    blocks = n // strips
    cs = cols // blocks
    hbm = pl.BlockSpec(memory_space=pltpu.HBM)
    smem = pl.BlockSpec(memory_space=pltpu.SMEM)
    dma = pltpu.SemaphoreType.DMA
    f32 = jnp.float32

    count = positions * dies
    chunks = cs // LANES
    pair = jnp.broadcast_to((slot_pos * dies + slot_die)[:, None], (slots, LANES))
    groups = positions // 4
    vmem = pltpu.VMEM
    refer = pl.pallas_call(
        functools.partial(refer_kernel, n, strips, blocks, cs, dies, positions),
        name="refer",
        out_shape=jax.ShapeDtypeStruct((strips, blocks, positions, RS, cs), f32),
        in_specs=[smem, smem, pl.BlockSpec(memory_space=pltpu.VMEM), hbm, hbm],
        out_specs=hbm,
        scratch_shapes=[
            tuple(vmem((n * slots, RS, LANES), f32) for _ in range(chunks)),
            vmem((positions, RS, cs), f32),
            vmem((n * slots, LANES), jnp.int32),
            vmem((count // LANES, LANES), jnp.int32),
            pltpu.SMEM((count // LANES, LANES), jnp.int32),
            vmem((ITERS, positions, RS, cs), f32),
            vmem((ITERS, groups, 8, cs), f32),
            vmem((ITERS, groups, 8, cs), f32),
            vmem((ITERS, groups, 8, cs), f32),
            vmem((ITERS, groups, 8, cs), f32),
            vmem((ITERS, positions, RS, LANES), f32),
            vmem((ITERS, positions, RS, LANES), f32),
            vmem((ITERS, 4, groups, 8, LANES), f32),
            vmem((4, 24, cs + 2 * LANES), f32),
            vmem((positions, RS, cs), f32),
            dma((chunks, n)),
            dma((chunks, n)),
            dma((n,)),
            dma((n,)),
            dma((n,)),
            dma((n,)),
            dma((3 + chunks,)),
            dma((ITERS, HALVES, 8)),
            dma((ITERS, HALVES, 8)),
            dma((strips, PARTS)),
            dma((strips, PARTS)),
            dma((strips, PARTS, blocks)),
            dma((strips, PARTS, blocks)),
            dma((PARTS,)),
        ],
        compiler_params=pltpu.CompilerParams(
            collective_id=0, has_side_effects=True, vmem_limit_bytes=56 * 1024 * 1024
        ),
    )(
        present.T.astype(f32).reshape(count),
        kernel.reshape(25),
        pair,
        die_tiles,
        strength,
    )

    return pl.pallas_call(
        functools.partial(residual_kernel, strips, blocks, cs),
        name="residual",
        out_shape=jax.ShapeDtypeStruct((slots, rows, cols), f32),
        grid_spec=pltpu.PrefetchScalarGridSpec(
            num_scalar_prefetch=3,
            grid=(slots // PER_STEP,),
            in_specs=[
                pl.BlockSpec((PER_STEP, rows, cols), lambda i, *_: (i, 0, 0)),
                *[refer_spec(strips, blocks, cs, u) for u in range(PER_STEP)],
            ],
            out_specs=pl.BlockSpec((PER_STEP, rows, cols), lambda i, *_: (i, 0, 0)),
        ),
        compiler_params=pltpu.CompilerParams(vmem_limit_bytes=56 * 1024 * 1024),
    )(slot_pos, slot_die, present, die_tiles, *[refer] * PER_STEP)


CUTS = (5, 8)
AHEAD = 2
BESIDE = 1
MESH_ID = pl.DeviceIdType.MESH


def fits(mesh, die_tiles, present, strength):
    n = mesh.shape["die"]
    slots, rows, cols = die_tiles
    dies, positions = present
    return (
        mesh.shape["wafer"] == 2
        and n == 2 * (rows // RS)
        and rows // RS % 4 == 0
        and cols == CUTS[-1] * LANES
        and strength[0] == 2
        and positions == n * 2
        and positions % 16 == 0
        and positions * dies % LANES == 0
    )


def strip_kernel(
    n, dies, present, kern, slot_pos, slot_die, tiles, power, out,
    stacks, strength, pair, pairs, table, where, mean, top, bottom, above, below, ext, refers, windows,
    fsend, frecv, flocal, rsend, rrecv, qsend, qrecv, qlocal, tsend, trecv, tlocal, xsend, xrecv,
    hsend, hrecv, usend, urecv, dsend, drecv, ysend, yrecv, csend, crecv, wload, wstore,
):
    me = lax.axis_index("die")
    wafer = lax.axis_index("wafer")
    chips = n // 2
    depth = chips // 2
    q, c = me // 2, me % 2
    z, y = q // 2, q % 2
    slots, rows, cols = tiles.shape
    per = strength.shape[0] * strength.shape[1]
    groups = per // 4
    blocks = len(stacks)
    phases = len(CUTS)
    ends = CUTS
    starts = (0,) + CUTS[:-1]
    shown = tuple(e - 1 for e in CUTS[:-1]) + (CUTS[-1],)
    hidden = (0,) + shown[:-1]

    def strip_at(zz, yy):
        return 2 * zz + yy * (1 - zz % 2) + (1 - yy) * (zz % 2)

    def chip_at(s):
        zz, odd = s // 2, s % 2
        return 2 * zz + odd * (1 - zz % 2) + (1 - odd) * (zz % 2)

    def lanes(a, b):
        return pl.ds(a * LANES, (b - a) * LANES)

    def rows_of(chip):
        return pl.ds(pl.multiple_of(strip_at(chip // 2, chip % 2) * RS, RS), RS)

    s = strip_at(z, y)
    other = 2 * q + 1 - c

    barrier = pltpu.get_barrier_semaphore()
    for k in range(1, n):
        pl.semaphore_signal(barrier, inc=1, device_id={"die": (me + k) % n}, device_id_type=MESH_ID)
    pl.semaphore_signal(barrier, inc=1, device_id={"wafer": 1 - wafer}, device_id_type=MESH_ID)
    for i in range(slots):
        pair[i : i + 1, :] = jnp.full((1, LANES), slot_pos[i] * dies + slot_die[i], jnp.int32)
    pl.semaphore_wait(barrier, n)

    ours = pl.ds((c * chips + q) * slots, slots)
    pair_copies = [pltpu.make_async_copy(pair, pairs.at[ours], qlocal)]
    for k in range(1, n):
        pair_copies.append(remote(pair, pairs.at[ours], qsend.at[k], qrecv.at[k], (me + k) % n))
    for copy in pair_copies:
        copy.start()

    waves = []
    for b in range(blocks):
        here = pltpu.make_async_copy(tiles.at[:, rows_of(q), lanes(b, b + 1)], stacks[b].at[ours], flocal.at[b])
        there = []
        for k in range(1, chips):
            chip = (q + k) % chips
            there.append(
                remote(
                    tiles.at[:, rows_of(chip), lanes(b, b + 1)], stacks[b].at[ours],
                    fsend.at[b, k], frecv.at[b, k], 2 * chip + c,
                )
            )
        waves.append((here, there))

    def issue(b):
        here, there = waves[b]
        here.start()
        for copy in there:
            copy.start()

    issued = []

    def pump(last, limit):
        while len(issued) <= min(last, limit - 1, blocks - 1):
            issue(len(issued))
            issued.append(True)

    half = pl.ds(c * chips * slots, chips * slots)
    relays = [remote(stacks[b].at[half], stacks[b].at[half], rsend.at[b], rrecv.at[b], other) for b in range(blocks)]

    plane, turn = me // chips, me % chips

    def power_copy(u, k):
        chip = (q + k) % chips
        src = power.at[wafer, rows_of(chip), lanes(starts[u], ends[u])]
        dst = strength.at[wafer, turn, :, lanes(starts[u], ends[u])]
        return src, dst, 2 * chip + plane

    def power_remote(u, k):
        src, dst, device = power_copy(u, k)
        return remote(src, dst, tsend.at[u, k], trecv.at[u, turn], device)

    def power_local(u):
        src, dst, _ = power_copy(u, 0)
        return pltpu.make_async_copy(src, dst, tlocal.at[u])

    def power_start(u):
        @pl.when(plane == c)
        def _():
            power_local(u).start()

        @pl.when(plane != c)
        def _():
            power_remote(u, 0).start()

        for k in range(1, chips):
            power_remote(u, k).start()

    def power_cross(u):
        part = strength.at[wafer, :, :, lanes(starts[u], ends[u])]
        return pltpu.make_async_remote_copy(
            src_ref=part, dst_ref=part, send_sem=xsend.at[u], recv_sem=xrecv.at[u],
            device_id={"wafer": 1 - wafer}, device_id_type=MESH_ID,
        )

    def power_pass(u):
        for t in range(chips):
            mine = c * chips + t == me

            @pl.when(mine)
            def _():
                power_local(u).wait()

            @pl.when(jnp.logical_not(mine))
            def _():
                part = strength.at[wafer, t, :, lanes(starts[u], ends[u])]
                remote(part, part, tsend.at[u, 0], trecv.at[u, t], other).wait_recv()

        power_cross(u).start()

    def power_end(u):
        power_cross(u).wait_send()
        part = strength.at[1 - wafer, :, :, lanes(starts[u], ends[u])]
        pltpu.make_async_remote_copy(
            src_ref=part, dst_ref=part, send_sem=xsend.at[u], recv_sem=xrecv.at[u],
            device_id={"wafer": 1 - wafer}, device_id_type=MESH_ID,
        ).wait_recv()

    def power_sent(u):
        @pl.when(plane != c)
        def _():
            power_remote(u, 0).wait_send()

        for k in range(1, chips):
            power_remote(u, k).wait_send()

    pump(0, blocks)
    power_start(0)
    pump(AHEAD - 1, blocks)

    loads = [
        pltpu.make_async_copy(tiles.at[:, :, lanes(hidden[u], shown[u])], windows[u], wload.at[u]) for u in range(phases)
    ]
    stores = [
        pltpu.make_async_copy(windows[u], out.at[:, :, lanes(hidden[u], shown[u])], wstore.at[u]) for u in range(phases)
    ]

    taps = [[kern[a, b] for b in range(5)] for a in range(5)]
    total = taps[0][0]
    for a in range(5):
        for b in range(5):
            if a or b:
                total = total + taps[a][b]

    def live(p, d):
        return present[d, p].astype(jnp.float32)

    def value_of(p, d, some):
        at = p * dies + d
        entry = where[at // LANES, at % LANES]
        if len(some) == 1:
            return stacks[some[0]][entry]
        return jnp.concatenate([stacks[b][entry] for b in some], axis=1)

    def huber(k, g, j, ref, some):
        span = lanes(some[0], some[-1] + 1)
        p = per * c + 4 * g + j
        num = None
        for d in range(dies):
            value = value_of(p, d, some)
            weight = live(p, d) / jnp.maximum(jnp.abs(value - ref), 1.5)
            num, den = (weight * value, weight) if num is None else (num + weight * value, den + weight)
        field = num / den
        mean[k, 4 * g + j, :, span] = field
        top[k, g, 2 * j : 2 * j + 2, span] = field[0:2]
        bottom[k, g, 2 * j : 2 * j + 2, span] = field[RS - 2 : RS]

    def guard(flag, x):
        return jnp.where(flag, x, jnp.zeros_like(x))

    has_up, has_down = s > 0, s < chips - 1

    def smooth(k, g, j, some, more):
        first, last = some[0], some[-1] + 1
        low = first - 1 if first else first
        high = last + 1 if more else last
        src = lanes(low, high)
        dst = lanes(low - first + 1, high - first + 1)
        width = (last - first + 2) * LANES
        rows2 = pl.ds(2 * j, 2)
        p = 4 * g + j
        ext[j, 6:8, dst] = guard(has_up, above[k, g, rows2, src])
        ext[j, 8:16, dst] = mean[k, p, :, src]
        ext[j, 16:18, dst] = guard(has_down, below[k, g, rows2, src])
        edge = jnp.zeros((24, LANES), jnp.float32)
        if not first:
            ext[j, :, 0:LANES] = edge
        if not more:
            ext[j, :, width - LANES : width] = edge
        shifted = [ext[j, 6 + a : 14 + a, 0:width] for a in range(5)]
        acc = None
        for b in range(5):
            part = shifted[0] * taps[0][b]
            for a in range(1, 5):
                part = part + shifted[a] * taps[a][b]
            if b != 2:
                part = pltpu.roll(part, (2 - b) % width, 1)
            part = part[:, LANES : width - LANES]
            acc = part if acc is None else acc + part
        field = mean[k, p, :, lanes(first, last)]
        power_p = strength[p % 2, p // 2, :, lanes(first, last)]
        return (field + power_p * acc) / (1.0 + power_p * total)

    def halo(u, k, h, start):
        first = starts[u] if k == 0 else hidden[u]
        span = lanes(first, ends[u])
        size = groups // HALVES
        g = pl.ds(h * size, size)
        down = remote(
            bottom.at[k, g, :, span], above.at[k, g, :, span], hsend.at[u, k, h, 0], hrecv.at[u, k, h, 0],
            2 * chip_at((s + 1) % chips) + c,
        )
        up = remote(
            top.at[k, g, :, span], below.at[k, g, :, span], hsend.at[u, k, h, 1], hrecv.at[u, k, h, 1],
            2 * chip_at((s + chips - 1) % chips) + c,
        )
        if start:

            @pl.when(has_down)
            def _():
                down.start()

            @pl.when(has_up)
            def _():
                up.start()

            return

        @pl.when(has_down)
        def _():
            down.wait_send()
            up.wait_recv()

        @pl.when(has_up)
        def _():
            up.wait_send()
            down.wait_recv()

    def part(u, zz, yy, cc):
        return refers[u].at[strip_at(zz, yy), pl.ds(cc * per, per)]

    def to_up(u, t):
        block = part(u, (z - t + depth) % depth, y, c)
        return remote(block, block, usend.at[u, t], urecv.at[u, t], (me + 4) % n)

    def to_down(u, t):
        block = part(u, (z + t) % depth, y, c)
        return remote(block, block, dsend.at[u, t], drecv.at[u, t], (me + n - 4) % n)

    def to_side(u, zz):
        block = part(u, zz, y, c)
        return remote(block, block, ysend.at[u, zz], yrecv.at[u, zz], 4 * z + 2 * (1 - y) + c)

    def to_core(u, zz, yy):
        block = part(u, zz, yy, c)
        return remote(block, block, csend.at[u, 2 * zz + yy], crecv.at[u, 2 * zz + yy], other)

    def show(u):
        @pl.when(z < depth - 1)
        def _():
            to_up(u, 0).start()

        @pl.when(z > 0)
        def _():
            to_down(u, 0).start()

        to_side(u, z).start()
        to_core(u, z, y).start()

    def hop(u, t):
        @pl.when(z - t >= 0)
        def _():
            block = part(u, (z - t + depth) % depth, y, c)
            remote(block, block, usend.at[u, t - 1], urecv.at[u, t - 1], other).wait_recv()
            if t < depth - 1:

                @pl.when(z < depth - 1)
                def _():
                    to_up(u, t).start()

            to_side(u, (z - t + depth) % depth).start()
            to_core(u, (z - t + depth) % depth, y).start()

        @pl.when(z + t <= depth - 1)
        def _():
            block = part(u, (z + t) % depth, y, c)
            remote(block, block, dsend.at[u, t - 1], drecv.at[u, t - 1], other).wait_recv()
            if t < depth - 1:

                @pl.when(z > 0)
                def _():
                    to_down(u, t).start()

            to_side(u, (z + t) % depth).start()
            to_core(u, (z + t) % depth, y).start()

    def sides(u):
        for t in range(depth):
            zz = (z + t) % depth
            block = part(u, zz, 1 - y, c)
            remote(block, block, ysend.at[u, zz], yrecv.at[u, zz], other).wait_recv()
            to_core(u, zz, 1 - y).start()

    def residual(u):
        for q2 in range(chips):
            block = part(u, q2 // 2, q2 % 2, 1 - c)
            remote(block, block, csend.at[u, q2], crecv.at[u, q2], other).wait_recv()
        loads[u].wait()

        @pl.loop(0, slots)
        def _(i):
            at = slot_pos[i]
            keep = present[slot_die[i], at].astype(jnp.float32)
            for strip in range(chips):
                span = pl.ds(strip * RS, RS)
                windows[u][i, span, :] = keep * (windows[u][i, span, :] - refers[u][strip, at])

        stores[u].start()

    def sent(u):
        for t in range(depth - 1):

            @pl.when((z < depth - 1) & (z - t >= 0))
            def _():
                to_up(u, t).wait_send()

            @pl.when((z > 0) & (z + t <= depth - 1))
            def _():
                to_down(u, t).wait_send()

        for zz in range(depth):
            to_side(u, zz).wait_send()
            for yy in range(2):
                to_core(u, zz, yy).wait_send()

    size = groups // HALVES
    for u in range(phases):
        fresh = tuple(range(starts[u], ends[u]))
        again = tuple(range(hidden[u], ends[u]))
        done = tuple(range(hidden[u], shown[u]))
        loads[u].start()
        for b in fresh:
            here, there = waves[b]
            here.wait()
            for copy in there:
                copy.wait_recv()
            relays[b].start()
            pump(b + AHEAD, ends[u] + BESIDE)
            if u + 1 < phases and b == fresh[0]:
                power_start(u + 1)
        if u == 0:
            for copy in pair_copies:
                copy.wait()
            order = lax.broadcasted_iota(jnp.int32, (n * slots, LANES), 0)
            target = lax.broadcasted_iota(jnp.int32, (n * slots, LANES), 1)
            for w in range(table.shape[0]):
                hit = pairs[...] == target + w * LANES
                table[w : w + 1, :] = jnp.max(jnp.where(hit, order, 0), axis=0, keepdims=True)
            fetch = pltpu.make_async_copy(table, where, qlocal)
            fetch.start()
            fetch.wait()
        power_pass(u)
        for b in fresh:
            part_b = stacks[b].at[pl.ds((1 - c) * chips * slots, chips * slots)]
            remote(part_b, part_b, rsend.at[b], rrecv.at[b], other).wait_recv()

        for h in range(HALVES):

            @pl.loop(h * size, (h + 1) * size)
            def _(g):
                for j in range(4):
                    p = per * c + 4 * g + j
                    count = live(p, 0)
                    num = count * value_of(p, 0, fresh)
                    for d in range(1, dies):
                        share = live(p, d)
                        count = count + share
                        num = num + share * value_of(p, d, fresh)
                    huber(0, g, j, num / jnp.full(num.shape, count), fresh)

            halo(u, 0, h, True)
        power_end(u)
        if u:
            hop(u - 1, 1)
        for k in range(1, ITERS):
            for h in range(HALVES):
                halo(u, k - 1, h, False)
                if h == HALVES - 1:
                    pump(blocks, len(issued) + 1)

                @pl.loop(h * size, (h + 1) * size)
                def _(g):
                    for j in range(4):
                        huber(k, g, j, smooth(k - 1, g, j, again, False), again)

                halo(u, k, h, True)
            if u:
                hop(u - 1, k + 1)
        for h in range(HALVES):
            halo(u, ITERS - 1, h, False)

            @pl.loop(h * size, (h + 1) * size)
            def _(g):
                for j in range(4):
                    value = smooth(ITERS - 1, g, j, done, done[-1] + 1 < ends[u])
                    refers[u][s, per * c + 4 * g + j] = value

        pump(blocks, len(issued) + 1)
        show(u)
        if u:
            sides(u - 1)
            residual(u - 1)
    for t in range(1, depth):
        hop(phases - 1, t)
    sides(phases - 1)
    residual(phases - 1)
    for b in range(blocks):
        for copy in waves[b][1]:
            copy.wait_send()
        relays[b].wait_send()
    for u in range(phases):
        power_sent(u)
        sent(u)
        stores[u].wait()


def strip_shards(n, die_tiles, slot_pos, slot_die, present, strength, kernel):
    slots, rows, cols = die_tiles.shape
    dies, positions = present.shape
    chips = n // 2
    depth = chips // 2
    per = positions // 2
    blocks = cols // LANES
    phases = len(CUTS)
    shown = [0] + [e - 1 for e in CUTS[:-1]] + [CUTS[-1]]
    widths = [(b - a) * LANES for a, b in zip(shown, shown[1:])]
    hbm = pl.BlockSpec(memory_space=pltpu.HBM)
    smem = pl.BlockSpec(memory_space=pltpu.SMEM)
    dma = pltpu.SemaphoreType.DMA
    vmem = pltpu.VMEM
    f32 = jnp.float32
    count = positions * dies
    edges = (ITERS, per // 4, 8, cols)
    return pl.pallas_call(
        functools.partial(strip_kernel, n, dies),
        name="strips",
        out_shape=jax.ShapeDtypeStruct((slots, rows, cols), f32),
        in_specs=[smem, smem, smem, smem, hbm, hbm],
        out_specs=hbm,
        scratch_shapes=[
            tuple(vmem((n * slots, RS, LANES), f32) for _ in range(blocks)),
            vmem((2, per // 2, RS, cols), f32),
            vmem((slots, LANES), jnp.int32),
            vmem((n * slots, LANES), jnp.int32),
            vmem((count // LANES, LANES), jnp.int32),
            pltpu.SMEM((count // LANES, LANES), jnp.int32),
            vmem((ITERS, per, RS, cols), f32),
            vmem(edges, f32),
            vmem(edges, f32),
            vmem(edges, f32),
            vmem(edges, f32),
            vmem((4, 24, cols + 2 * LANES), f32),
            tuple(vmem((chips, positions, RS, w), f32) for w in widths),
            tuple(vmem((slots, rows, w), f32) for w in widths),
            dma((blocks, chips)),
            dma((blocks, chips)),
            dma((blocks,)),
            dma((blocks,)),
            dma((blocks,)),
            dma((n,)),
            dma((n,)),
            dma,
            dma((phases, chips)),
            dma((phases, chips)),
            dma((phases,)),
            dma((phases,)),
            dma((phases,)),
            dma((phases, ITERS, HALVES, 2)),
            dma((phases, ITERS, HALVES, 2)),
            dma((phases, depth)),
            dma((phases, depth)),
            dma((phases, depth)),
            dma((phases, depth)),
            dma((phases, depth)),
            dma((phases, depth)),
            dma((phases, chips)),
            dma((phases, chips)),
            dma((phases,)),
            dma((phases,)),
        ],
        compiler_params=pltpu.CompilerParams(
            collective_id=1, has_side_effects=True, vmem_limit_bytes=56 * 1024 * 1024
        ),
    )(present, kernel, slot_pos, slot_die, die_tiles, strength)


def either(mesh, die_tiles, slot_pos, slot_die, present, strength, kernel):
    n = mesh.shape["die"]
    run = strip_shards if fits(mesh, die_tiles.shape, present.shape, strength.shape) else shards
    return run(n, die_tiles, slot_pos, slot_die, present, strength, kernel)


def solution(mesh):
    placed = (
        P(("wafer", "die"), None, None),
        P(("wafer", "die")),
        P(("wafer", "die")),
        P("wafer", None),
        P("die", None, None),
        P(),
    )
    return jax.shard_map(
        functools.partial(either, mesh),
        mesh=mesh,
        in_specs=placed,
        out_specs=P(("wafer", "die"), None, None),
        check_vma=False,
    )
```

```python
import functools

import jax
import jax.numpy as jnp
from jax import lax
from jax.experimental import pallas as pl
from jax.experimental.pallas import tpu as pltpu
from jax.sharding import PartitionSpec as P

ITERS = 3
RS = 8
LANES = 128
PARTS = 4
HALVES = 2
PER_STEP = 2


def strip_of(q, strips):
    odd = q % 2
    half = q // 2
    return half * (1 - odd) + (strips - 1 - half) * odd


def chip_of(s, strips):
    high = s // (strips // 2)
    return 2 * s * (1 - high) + (2 * (strips - 1 - s) + 1) * high


def greet(n):
    me = lax.axis_index("die")
    barrier = pltpu.get_barrier_semaphore()
    for k in range(1, n):
        pl.semaphore_signal(barrier, inc=1, device_id={"die": (me + k) % n}, device_id_type=pl.DeviceIdType.MESH)
    pl.semaphore_wait(barrier, n - 1)


def remote(src, dst, send, recv, device):
    return pltpu.make_async_remote_copy(
        src_ref=src, dst_ref=dst, send_sem=send, recv_sem=recv,
        device_id={"die": device}, device_id_type=pl.DeviceIdType.MESH,
    )


def refer_kernel(
    n, strips, blocks, cs, dies, positions,
    live, kern, pair, tiles, power, out,
    stacks, strength, pairs, table, where, mean,
    top, bottom, rows_up, rows_down, side_left, side_right, corners, ext, refer,
    send, recv, psend, precv, qsend, qrecv, local, hsend, hrecv, rsend, rrecv, ssend, srecv, own,
):
    me = lax.axis_index("die")
    slots = tiles.shape[0]
    held = power.shape[0]
    chunks = cs // LANES
    s = strip_of(me // blocks, strips)
    c = me % blocks
    groups = positions // 4

    def device(ds, dc):
        return chip_of((s + ds + strips) % strips, strips) * blocks + (c + dc + blocks) % blocks

    def rows_of(peer):
        return pl.ds(pl.multiple_of(strip_of(peer // blocks, strips) * RS, RS), RS)

    def cols_of(peer, start, size):
        return pl.ds(pl.multiple_of((peer % blocks) * cs + start, LANES), size)

    tile_rows = pl.ds(me * slots, slots)
    power_rows = pl.ds(me * held, held)
    greet(n)
    pair_copies = [pltpu.make_async_copy(pair, pairs.at[tile_rows], local.at[0])]
    for k in range(1, n):
        pair_copies.append(remote(pair, pairs.at[tile_rows], qsend.at[k], qrecv.at[k], (me + k) % n))
    for copy in pair_copies:
        copy.start()
    tile_copies = []
    for u in range(chunks):
        wave = [
            pltpu.make_async_copy(
                tiles.at[:, rows_of(me), cols_of(me, u * LANES, LANES)], stacks[u].at[tile_rows], local.at[2 + u]
            )
        ]
        for k in range(1, n):
            peer = (me + k) % n
            wave.append(
                remote(
                    tiles.at[:, rows_of(peer), cols_of(peer, u * LANES, LANES)], stacks[u].at[tile_rows],
                    send.at[u, k], recv.at[u, k], peer,
                )
            )
        for copy in wave:
            copy.start()
        tile_copies.append(wave)
    power_copies = [
        pltpu.make_async_copy(power.at[:, rows_of(me), cols_of(me, 0, cs)], strength.at[power_rows], local.at[1])
    ]
    for k in range(1, n):
        peer = (me + k) % n
        power_copies.append(
            remote(
                power.at[:, rows_of(peer), cols_of(peer, 0, cs)], strength.at[power_rows],
                psend.at[k], precv.at[k], peer,
            )
        )
    for copy in power_copies:
        copy.start()

    for copy in pair_copies:
        copy.wait()
    order = lax.broadcasted_iota(jnp.int32, (n * slots, LANES), 0)
    target = lax.broadcasted_iota(jnp.int32, (n * slots, LANES), 1)
    for w in range(table.shape[0]):
        hit = pairs[...] == target + w * LANES
        table[w : w + 1, :] = jnp.max(jnp.where(hit, order, 0), axis=0, keepdims=True)
    fetch = pltpu.make_async_copy(table, where, local.at[2 + chunks])
    fetch.start()
    fetch.wait()

    def value_of(p, d, some):
        q = p * dies + d
        entry = where[q // LANES, q % LANES]
        if len(some) == 1:
            return stacks[some[0]][entry]
        return jnp.concatenate([stacks[u][entry] for u in some], axis=1)

    first = pl.ds(0, LANES)
    last = pl.ds(cs - LANES, LANES)
    taps = [[kern[5 * a + b] for b in range(5)] for a in range(5)]
    total = taps[0][0]
    for a in range(5):
        for b in range(5):
            if a or b:
                total = total + taps[a][b]

    def exchange(k, h):
        size = groups // HALVES
        g = pl.ds(h * size, size)
        p = pl.ds(h * size * 4, size * 4)
        moves = [
            (bottom.at[k, g], rows_up.at[k, g], 1, 0),
            (top.at[k, g], rows_down.at[k, g], -1, 0),
            (mean.at[k, p, :, last], side_left.at[k, p], 0, 1),
            (mean.at[k, p, :, first], side_right.at[k, p], 0, -1),
            (bottom.at[k, g, :, last], corners.at[k, 0, g], 1, 1),
            (bottom.at[k, g, :, first], corners.at[k, 1, g], 1, -1),
            (top.at[k, g, :, last], corners.at[k, 2, g], -1, 1),
            (top.at[k, g, :, first], corners.at[k, 3, g], -1, -1),
        ]
        copies = [
            remote(src, dst, hsend.at[k, h, m], hrecv.at[k, h, m], device(ds, dc))
            for m, (src, dst, ds, dc) in enumerate(moves)
        ]
        for copy in copies:
            copy.start()
        return copies

    def guard(flag, x):
        return jnp.where(flag, x, jnp.zeros_like(x))

    has_up, has_down, has_left, has_right = s > 0, s < strips - 1, c > 0, c < blocks - 1
    body = pl.ds(LANES, cs)
    right = pl.ds(LANES + cs, LANES)

    def smooth(k, g, j):
        p = 4 * g + j
        pair = pl.ds(2 * j, 2)
        field = mean[k, p]
        ext[j, 6:8, first] = guard(has_up & has_left, corners[k, 0, g, pair, :])
        ext[j, 6:8, body] = guard(has_up, rows_up[k, g, pair, :])
        ext[j, 6:8, right] = guard(has_up & has_right, corners[k, 1, g, pair, :])
        ext[j, 8:16, first] = guard(has_left, side_left[k, p])
        ext[j, 8:16, body] = field
        ext[j, 8:16, right] = guard(has_right, side_right[k, p])
        ext[j, 16:18, first] = guard(has_down & has_left, corners[k, 2, g, pair, :])
        ext[j, 16:18, body] = guard(has_down, rows_down[k, g, pair, :])
        ext[j, 16:18, right] = guard(has_down & has_right, corners[k, 3, g, pair, :])
        shifted = [ext[j, 6 + a : 14 + a, :] for a in range(5)]
        width = cs + 2 * LANES
        acc = None
        for b in range(5):
            part = shifted[0] * taps[0][b]
            for a in range(1, 5):
                part = part + shifted[a] * taps[a][b]
            if b != 2:
                part = pltpu.roll(part, (2 - b) % width, 1)
            part = part[:, LANES : LANES + cs]
            acc = part if acc is None else acc + part
        power_p = strength[p]
        return (field + power_p * acc) / (1.0 + power_p * total)

    def huber(k, g, j, ref, some):
        lanes = pl.ds(some[0] * LANES, len(some) * LANES)
        p = 4 * g + j
        num = None
        for d in range(dies):
            value = value_of(p, d, some)
            weight = live[p * dies + d] / jnp.maximum(jnp.abs(value - ref), 1.5)
            num, den = (weight * value, weight) if num is None else (num + weight * value, den + weight)
        field = num / den
        mean[k, p, :, lanes] = field
        top[k, g, 2 * j : 2 * j + 2, lanes] = field[0:2]
        bottom[k, g, 2 * j : 2 * j + 2, lanes] = field[RS - 2 : RS]

    for u in range(chunks):
        some = (u,)
        for copy in tile_copies[u]:
            copy.wait()

        @pl.loop(0, groups)
        def _(g):
            for j in range(4):
                p = 4 * g + j
                count = live[p * dies]
                num = count * value_of(p, 0, some)
                for d in range(1, dies):
                    share = live[p * dies + d]
                    count = count + share
                    num = num + share * value_of(p, d, some)
                huber(0, g, j, num / jnp.full(num.shape, count), some)

    halo = [exchange(0, h) for h in range(HALVES)]
    for copy in power_copies:
        copy.wait()
    for k in range(1, ITERS):
        later = []
        for h in range(HALVES):
            for copy in halo[h]:
                copy.wait()

            @pl.loop(h * groups // HALVES, (h + 1) * groups // HALVES)
            def _(g):
                for j in range(4):
                    huber(k, g, j, smooth(k - 1, g, j), tuple(range(chunks)))

            later.append(exchange(k, h))
        halo = later

    turn = 1 - 2 * (c % 2)
    ahead = device(turn, 0)
    parts = rsend.shape[1]
    span = positions // parts
    pending = []
    rings = {}
    mine = []

    def forward(t, h):
        strip = (s - turn * t + strips) % strips
        part = pl.ds(h * span, span)
        target = out.at[strip, c, part]
        block = target if t else refer.at[part]
        if t:
            rings[t - 1, h].wait_recv()
        copies = [remote(block, target, ssend.at[t, h, b], srecv.at[t, h, b], device(0, b)) for b in range(1, blocks)]
        if t < strips - 1:
            rings[t, h] = remote(block, target, rsend.at[t, h], rrecv.at[t, h], ahead)
            copies.insert(0, rings[t, h])
        for copy in copies:
            copy.start()
        pending.extend(copies)

    for h in range(parts):
        if h * HALVES % parts == 0:
            for copy in halo[h * HALVES // parts]:
                copy.wait()

        @pl.loop(h * span // 4, (h + 1) * span // 4)
        def _(g):
            for j in range(4):
                refer[4 * g + j] = smooth(ITERS - 1, g, j)

        part = pl.ds(h * span, span)
        mine.append(pltpu.make_async_copy(refer.at[part], out.at[s, c, part], own.at[h]))
        mine[-1].start()
        forward(0, h)
    for t in range(1, strips):
        for h in range(parts):
            forward(t, h)
    for copy in pending:
        copy.wait_send()
    for t in range(strips):
        for h in range(parts):
            for b in range(1, blocks):
                source = (c - b + blocks) % blocks
                strip = (s - (1 - 2 * (source % 2)) * t + strips) % strips
                target = out.at[strip, source, pl.ds(h * span, span)]
                remote(target, target, ssend.at[t, h, b], srecv.at[t, h, b], device(0, b)).wait_recv()
    for copy in mine:
        copy.wait()


def residual_kernel(strips, blocks, cs, pos, die, present, tile, *rest):
    out = rest[-1]
    for u in range(PER_STEP):
        slot = pl.program_id(0) * PER_STEP + u
        keep = present[die[slot], pos[slot]].astype(jnp.float32)
        for s in range(strips):
            for c in range(blocks):
                rows, cols = pl.ds(s * RS, RS), pl.ds(c * cs, cs)
                out[u, rows, cols] = keep * (tile[u, rows, cols] - rest[u][s, c, 0])


def refer_spec(strips, blocks, cs, u):
    return pl.BlockSpec((strips, blocks, 1, RS, cs), lambda i, pos, *_: (0, 0, pos[i * PER_STEP + u], 0, 0))


def shards(n, die_tiles, slot_pos, slot_die, present, strength, kernel):
    slots, rows, cols = die_tiles.shape
    dies, positions = present.shape
    strips = rows // RS
    blocks = n // strips
    cs = cols // blocks
    hbm = pl.BlockSpec(memory_space=pltpu.HBM)
    smem = pl.BlockSpec(memory_space=pltpu.SMEM)
    dma = pltpu.SemaphoreType.DMA
    f32 = jnp.float32

    count = positions * dies
    chunks = cs // LANES
    pair = jnp.broadcast_to((slot_pos * dies + slot_die)[:, None], (slots, LANES))
    groups = positions // 4
    vmem = pltpu.VMEM
    refer = pl.pallas_call(
        functools.partial(refer_kernel, n, strips, blocks, cs, dies, positions),
        name="refer",
        out_shape=jax.ShapeDtypeStruct((strips, blocks, positions, RS, cs), f32),
        in_specs=[smem, smem, pl.BlockSpec(memory_space=pltpu.VMEM), hbm, hbm],
        out_specs=hbm,
        scratch_shapes=[
            tuple(vmem((n * slots, RS, LANES), f32) for _ in range(chunks)),
            vmem((positions, RS, cs), f32),
            vmem((n * slots, LANES), jnp.int32),
            vmem((count // LANES, LANES), jnp.int32),
            pltpu.SMEM((count // LANES, LANES), jnp.int32),
            vmem((ITERS, positions, RS, cs), f32),
            vmem((ITERS, groups, 8, cs), f32),
            vmem((ITERS, groups, 8, cs), f32),
            vmem((ITERS, groups, 8, cs), f32),
            vmem((ITERS, groups, 8, cs), f32),
            vmem((ITERS, positions, RS, LANES), f32),
            vmem((ITERS, positions, RS, LANES), f32),
            vmem((ITERS, 4, groups, 8, LANES), f32),
            vmem((4, 24, cs + 2 * LANES), f32),
            vmem((positions, RS, cs), f32),
            dma((chunks, n)),
            dma((chunks, n)),
            dma((n,)),
            dma((n,)),
            dma((n,)),
            dma((n,)),
            dma((3 + chunks,)),
            dma((ITERS, HALVES, 8)),
            dma((ITERS, HALVES, 8)),
            dma((strips, PARTS)),
            dma((strips, PARTS)),
            dma((strips, PARTS, blocks)),
            dma((strips, PARTS, blocks)),
            dma((PARTS,)),
        ],
        compiler_params=pltpu.CompilerParams(
            collective_id=0, has_side_effects=True, vmem_limit_bytes=56 * 1024 * 1024
        ),
    )(
        present.T.astype(f32).reshape(count),
        kernel.reshape(25),
        pair,
        die_tiles,
        strength,
    )

    return pl.pallas_call(
        functools.partial(residual_kernel, strips, blocks, cs),
        name="residual",
        out_shape=jax.ShapeDtypeStruct((slots, rows, cols), f32),
        grid_spec=pltpu.PrefetchScalarGridSpec(
            num_scalar_prefetch=3,
            grid=(slots // PER_STEP,),
            in_specs=[
                pl.BlockSpec((PER_STEP, rows, cols), lambda i, *_: (i, 0, 0)),
                *[refer_spec(strips, blocks, cs, u) for u in range(PER_STEP)],
            ],
            out_specs=pl.BlockSpec((PER_STEP, rows, cols), lambda i, *_: (i, 0, 0)),
        ),
        compiler_params=pltpu.CompilerParams(vmem_limit_bytes=56 * 1024 * 1024),
    )(slot_pos, slot_die, present, die_tiles, *[refer] * PER_STEP)


CUTS = (5, 8)
AHEAD = 6
BESIDE = 3
UNITS = 2
MESH_ID = pl.DeviceIdType.MESH


def fits(mesh, die_tiles, present, strength):
    n = mesh.shape["die"]
    slots, rows, cols = die_tiles
    dies, positions = present
    return (
        mesh.shape["wafer"] == 2
        and n == 2 * (rows // RS)
        and rows // RS % 4 == 0
        and cols == CUTS[-1] * LANES
        and strength[0] == 2
        and positions == n * 2
        and positions % 16 == 0
        and positions * dies % LANES == 0
    )


def strip_kernel(
    n, dies, present, kern, slot_pos, slot_die, tiles, power, out,
    stacks, strength, pair, pairs, table, where, mean, top, bottom, above, below, ext, refers, windows,
    fsend, frecv, flocal, rsend, rrecv, qsend, qrecv, qlocal, tsend, trecv, tlocal, xsend, xrecv,
    hsend, hrecv, usend, urecv, dsend, drecv, ysend, yrecv, csend, crecv, wload, wstore,
):
    me = lax.axis_index("die")
    wafer = lax.axis_index("wafer")
    chips = n // 2
    depth = chips // 2
    q, c = me // 2, me % 2
    z, y = q // 2, q % 2
    slots, rows, cols = tiles.shape
    per = strength.shape[0] * strength.shape[1]
    groups = per // 4
    blocks = len(stacks)
    phases = len(CUTS)
    ends = CUTS
    starts = (0,) + CUTS[:-1]
    shown = tuple(e - 1 for e in CUTS[:-1]) + (CUTS[-1],)
    hidden = (0,) + shown[:-1]

    def strip_at(zz, yy):
        return 2 * zz + yy * (1 - zz % 2) + (1 - yy) * (zz % 2)

    def chip_at(s):
        zz, odd = s // 2, s % 2
        return 2 * zz + odd * (1 - zz % 2) + (1 - odd) * (zz % 2)

    def lanes(a, b):
        return pl.ds(a * LANES, (b - a) * LANES)

    def rows_of(chip):
        return pl.ds(pl.multiple_of(strip_at(chip // 2, chip % 2) * RS, RS), RS)

    s = strip_at(z, y)
    other = 2 * q + 1 - c

    barrier = pltpu.get_barrier_semaphore()
    for k in range(1, n):
        pl.semaphore_signal(barrier, inc=1, device_id={"die": (me + k) % n}, device_id_type=MESH_ID)
    pl.semaphore_signal(barrier, inc=1, device_id={"wafer": 1 - wafer}, device_id_type=MESH_ID)
    for i in range(slots):
        pair[i : i + 1, :] = jnp.full((1, LANES), slot_pos[i] * dies + slot_die[i], jnp.int32)
    pl.semaphore_wait(barrier, n)

    ours = pl.ds((c * chips + q) * slots, slots)
    pair_copies = [pltpu.make_async_copy(pair, pairs.at[ours], qlocal)]
    for k in range(1, n):
        pair_copies.append(remote(pair, pairs.at[ours], qsend.at[k], qrecv.at[k], (me + k) % n))
    for copy in pair_copies:
        copy.start()

    few = slots // UNITS
    waves = []
    for b in range(blocks):
        for e in range(UNITS):
            some = pl.ds(e * few, few)
            rows_in = pl.ds((c * chips + q) * slots + e * few, few)
            here = pltpu.make_async_copy(
                tiles.at[some, rows_of(q), lanes(b, b + 1)], stacks[b].at[rows_in], flocal.at[b, e]
            )
            there = []
            for k in range(1, chips):
                chip = (q + k) % chips
                there.append(
                    remote(
                        tiles.at[some, rows_of(chip), lanes(b, b + 1)], stacks[b].at[rows_in],
                        fsend.at[b, e, k], frecv.at[b, e, k], 2 * chip + c,
                    )
                )
            waves.append((here, there))
    issued = []

    def pump(last, limit):
        while len(issued) <= min(last, limit - 1, len(waves) - 1):
            here, there = waves[len(issued)]
            issued.append(True)
            here.start()
            for copy in there:
                copy.start()

    half = pl.ds(c * chips * slots, chips * slots)
    relays = [remote(stacks[b].at[half], stacks[b].at[half], rsend.at[b], rrecv.at[b], other) for b in range(blocks)]

    plane, turn = me // chips, me % chips

    def power_copy(u, k):
        chip = (q + k) % chips
        src = power.at[wafer, rows_of(chip), lanes(starts[u], ends[u])]
        dst = strength.at[wafer, turn, :, lanes(starts[u], ends[u])]
        return src, dst, 2 * chip + plane

    def power_remote(u, k):
        src, dst, device = power_copy(u, k)
        return remote(src, dst, tsend.at[u, k], trecv.at[u, turn], device)

    def power_local(u):
        src, dst, _ = power_copy(u, 0)
        return pltpu.make_async_copy(src, dst, tlocal.at[u])

    def power_start(u):
        @pl.when(plane == c)
        def _():
            power_local(u).start()

        @pl.when(plane != c)
        def _():
            power_remote(u, 0).start()

        for k in range(1, chips):
            power_remote(u, k).start()

    def power_cross(u):
        part = strength.at[wafer, :, :, lanes(starts[u], ends[u])]
        return pltpu.make_async_remote_copy(
            src_ref=part, dst_ref=part, send_sem=xsend.at[u], recv_sem=xrecv.at[u],
            device_id={"wafer": 1 - wafer}, device_id_type=MESH_ID,
        )

    def power_pass(u):
        for t in range(chips):
            mine = c * chips + t == me

            @pl.when(mine)
            def _():
                power_local(u).wait()

            @pl.when(jnp.logical_not(mine))
            def _():
                part = strength.at[wafer, t, :, lanes(starts[u], ends[u])]
                remote(part, part, tsend.at[u, 0], trecv.at[u, t], other).wait_recv()

        power_cross(u).start()

    def power_end(u):
        power_cross(u).wait_send()
        part = strength.at[1 - wafer, :, :, lanes(starts[u], ends[u])]
        pltpu.make_async_remote_copy(
            src_ref=part, dst_ref=part, send_sem=xsend.at[u], recv_sem=xrecv.at[u],
            device_id={"wafer": 1 - wafer}, device_id_type=MESH_ID,
        ).wait_recv()

    def power_sent(u):
        @pl.when(plane != c)
        def _():
            power_remote(u, 0).wait_send()

        for k in range(1, chips):
            power_remote(u, k).wait_send()

    pump(UNITS - 1, len(waves))
    power_start(0)
    pump(AHEAD - 1, len(waves))

    loads = [
        pltpu.make_async_copy(tiles.at[:, :, lanes(hidden[u], shown[u])], windows[u], wload.at[u]) for u in range(phases)
    ]
    stores = [
        pltpu.make_async_copy(windows[u], out.at[:, :, lanes(hidden[u], shown[u])], wstore.at[u]) for u in range(phases)
    ]

    taps = [[kern[a, b] for b in range(5)] for a in range(5)]
    total = taps[0][0]
    for a in range(5):
        for b in range(5):
            if a or b:
                total = total + taps[a][b]

    def live(p, d):
        return present[d, p].astype(jnp.float32)

    def value_of(p, d, some):
        at = p * dies + d
        entry = where[at // LANES, at % LANES]
        if len(some) == 1:
            return stacks[some[0]][entry]
        return jnp.concatenate([stacks[b][entry] for b in some], axis=1)

    def huber(k, g, j, ref, some):
        span = lanes(some[0], some[-1] + 1)
        p = per * c + 4 * g + j
        num = None
        for d in range(dies):
            value = value_of(p, d, some)
            weight = live(p, d) / jnp.maximum(jnp.abs(value - ref), 1.5)
            num, den = (weight * value, weight) if num is None else (num + weight * value, den + weight)
        field = num / den
        mean[k, 4 * g + j, :, span] = field
        top[k, g, 2 * j : 2 * j + 2, span] = field[0:2]
        bottom[k, g, 2 * j : 2 * j + 2, span] = field[RS - 2 : RS]

    def guard(flag, x):
        return jnp.where(flag, x, jnp.zeros_like(x))

    has_up, has_down = s > 0, s < chips - 1

    def smooth(k, g, j, some, more):
        first, last = some[0], some[-1] + 1
        low = first - 1 if first else first
        high = last + 1 if more else last
        src = lanes(low, high)
        dst = lanes(low - first + 1, high - first + 1)
        width = (last - first + 2) * LANES
        rows2 = pl.ds(2 * j, 2)
        p = 4 * g + j
        ext[j, 6:8, dst] = guard(has_up, above[k, g, rows2, src])
        ext[j, 8:16, dst] = mean[k, p, :, src]
        ext[j, 16:18, dst] = guard(has_down, below[k, g, rows2, src])
        edge = jnp.zeros((24, LANES), jnp.float32)
        if not first:
            ext[j, :, 0:LANES] = edge
        if not more:
            ext[j, :, width - LANES : width] = edge
        shifted = [ext[j, 6 + a : 14 + a, 0:width] for a in range(5)]
        acc = None
        for b in range(5):
            part = shifted[0] * taps[0][b]
            for a in range(1, 5):
                part = part + shifted[a] * taps[a][b]
            if b != 2:
                part = pltpu.roll(part, (2 - b) % width, 1)
            part = part[:, LANES : width - LANES]
            acc = part if acc is None else acc + part
        field = mean[k, p, :, lanes(first, last)]
        power_p = strength[p % 2, p // 2, :, lanes(first, last)]
        return (field + power_p * acc) / (1.0 + power_p * total)

    def halo(u, k, h, start):
        first = starts[u] if k == 0 else hidden[u]
        span = lanes(first, ends[u])
        size = groups // HALVES
        g = pl.ds(h * size, size)
        down = remote(
            bottom.at[k, g, :, span], above.at[k, g, :, span], hsend.at[u, k, h, 0], hrecv.at[u, k, h, 0],
            2 * chip_at((s + 1) % chips) + c,
        )
        up = remote(
            top.at[k, g, :, span], below.at[k, g, :, span], hsend.at[u, k, h, 1], hrecv.at[u, k, h, 1],
            2 * chip_at((s + chips - 1) % chips) + c,
        )
        if start:

            @pl.when(has_down)
            def _():
                down.start()

            @pl.when(has_up)
            def _():
                up.start()

            return

        @pl.when(has_down)
        def _():
            down.wait_send()
            up.wait_recv()

        @pl.when(has_up)
        def _():
            up.wait_send()
            down.wait_recv()

    def part(v, zz, yy, cc):
        u, h = v // HALVES, v % HALVES
        return refers[u].at[strip_at(zz, yy), pl.ds(cc * per + h * (per // HALVES), per // HALVES)]

    def to_up(u, t):
        block = part(u, (z - t + depth) % depth, y, c)
        return remote(block, block, usend.at[u, t], urecv.at[u, t], (me + 4) % n)

    def to_down(u, t):
        block = part(u, (z + t) % depth, y, c)
        return remote(block, block, dsend.at[u, t], drecv.at[u, t], (me + n - 4) % n)

    def to_side(u, zz):
        block = part(u, zz, y, c)
        return remote(block, block, ysend.at[u, zz], yrecv.at[u, zz], 4 * z + 2 * (1 - y) + c)

    def to_core(u, zz, yy):
        block = part(u, zz, yy, c)
        return remote(block, block, csend.at[u, 2 * zz + yy], crecv.at[u, 2 * zz + yy], other)

    def show(u):
        @pl.when(z < depth - 1)
        def _():
            to_up(u, 0).start()

        @pl.when(z > 0)
        def _():
            to_down(u, 0).start()

        to_side(u, z).start()
        to_core(u, z, y).start()

    def hop(u, t):
        @pl.when(z - t >= 0)
        def _():
            block = part(u, (z - t + depth) % depth, y, c)
            remote(block, block, usend.at[u, t - 1], urecv.at[u, t - 1], other).wait_recv()
            if t < depth - 1:

                @pl.when(z < depth - 1)
                def _():
                    to_up(u, t).start()

            to_side(u, (z - t + depth) % depth).start()
            to_core(u, (z - t + depth) % depth, y).start()

        @pl.when(z + t <= depth - 1)
        def _():
            block = part(u, (z + t) % depth, y, c)
            remote(block, block, dsend.at[u, t - 1], drecv.at[u, t - 1], other).wait_recv()
            if t < depth - 1:

                @pl.when(z > 0)
                def _():
                    to_down(u, t).start()

            to_side(u, (z + t) % depth).start()
            to_core(u, (z + t) % depth, y).start()

    def hops(u, t):
        for v in range(max(u, 0) * HALVES, (u + 1) * HALVES):
            hop(v, t)

    def sides(u):
        for t in range(depth):
            zz = (z + t) % depth
            block = part(u, zz, 1 - y, c)
            remote(block, block, ysend.at[u, zz], yrecv.at[u, zz], other).wait_recv()
            to_core(u, zz, 1 - y).start()

    def residual(u):
        for v in range(u * HALVES, (u + 1) * HALVES):
            for q2 in range(chips):
                block = part(v, q2 // 2, q2 % 2, 1 - c)
                remote(block, block, csend.at[v, q2], crecv.at[v, q2], other).wait_recv()
        loads[u].wait()

        @pl.loop(0, slots)
        def _(i):
            at = slot_pos[i]
            keep = present[slot_die[i], at].astype(jnp.float32)
            for strip in range(chips):
                span = pl.ds(strip * RS, RS)
                windows[u][i, span, :] = keep * (windows[u][i, span, :] - refers[u][strip, at])

        stores[u].start()

    def sent(u):
        for t in range(depth - 1):

            @pl.when((z < depth - 1) & (z - t >= 0))
            def _():
                to_up(u, t).wait_send()

            @pl.when((z > 0) & (z + t <= depth - 1))
            def _():
                to_down(u, t).wait_send()

        for zz in range(depth):
            to_side(u, zz).wait_send()
            for yy in range(2):
                to_core(u, zz, yy).wait_send()

    size = groups // HALVES
    for u in range(phases):
        fresh = tuple(range(starts[u], ends[u]))
        again = tuple(range(hidden[u], ends[u]))
        done = tuple(range(hidden[u], shown[u]))
        loads[u].start()
        for b in fresh:
            for e in range(b * UNITS, (b + 1) * UNITS):
                here, there = waves[e]
                here.wait()
                for copy in there:
                    copy.wait_recv()
                pump(e + AHEAD, ends[u] * UNITS + BESIDE)
            relays[b].start()
            if u + 1 < phases and b == fresh[0]:
                power_start(u + 1)
        if u == 0:
            for copy in pair_copies:
                copy.wait()
            order = lax.broadcasted_iota(jnp.int32, (n * slots, LANES), 0)
            target = lax.broadcasted_iota(jnp.int32, (n * slots, LANES), 1)
            for w in range(table.shape[0]):
                hit = pairs[...] == target + w * LANES
                table[w : w + 1, :] = jnp.max(jnp.where(hit, order, 0), axis=0, keepdims=True)
            fetch = pltpu.make_async_copy(table, where, qlocal)
            fetch.start()
            fetch.wait()
        power_pass(u)
        for b in fresh:
            part_b = stacks[b].at[pl.ds((1 - c) * chips * slots, chips * slots)]
            remote(part_b, part_b, rsend.at[b], rrecv.at[b], other).wait_recv()

        for h in range(HALVES):

            @pl.loop(h * size, (h + 1) * size)
            def _(g):
                for j in range(4):
                    p = per * c + 4 * g + j
                    count = live(p, 0)
                    num = count * value_of(p, 0, fresh)
                    for d in range(1, dies):
                        share = live(p, d)
                        count = count + share
                        num = num + share * value_of(p, d, fresh)
                    huber(0, g, j, num / jnp.full(num.shape, count), fresh)

            halo(u, 0, h, True)
        power_end(u)
        hops(u - 1, 1)
        if u > 1:
            for v in range((u - 2) * HALVES, (u - 1) * HALVES):
                sides(v)
        for k in range(1, ITERS):
            for h in range(HALVES):
                halo(u, k - 1, h, False)
                pump(len(waves), len(issued) + 1)

                @pl.loop(h * size, (h + 1) * size)
                def _(g):
                    for j in range(4):
                        huber(k, g, j, smooth(k - 1, g, j, again, False), again)

                halo(u, k, h, True)
            hops(u - 1, k + 1)
            if u > 1 and k == 1:
                residual(u - 2)
        for h in range(HALVES):
            halo(u, ITERS - 1, h, False)

            @pl.loop(h * size, (h + 1) * size)
            def _(g):
                for j in range(4):
                    value = smooth(ITERS - 1, g, j, done, done[-1] + 1 < ends[u])
                    refers[u][s, per * c + 4 * g + j] = value

            show(u * HALVES + h)
        pump(len(waves), len(issued) + 1)
    u = phases - 1
    hops(u, 1)
    for v in range((u - 1) * HALVES, u * HALVES):
        sides(v)
    hops(u, 2)
    residual(u - 1)
    hops(u, 3)
    for v in range(u * HALVES, (u + 1) * HALVES):
        sides(v)
    residual(u)
    for here, there in waves:
        for copy in there:
            copy.wait_send()
    for copy in relays:
        copy.wait_send()
    for u in range(phases):
        power_sent(u)
        for v in range(u * HALVES, (u + 1) * HALVES):
            sent(v)
        stores[u].wait()


def strip_shards(n, die_tiles, slot_pos, slot_die, present, strength, kernel):
    slots, rows, cols = die_tiles.shape
    dies, positions = present.shape
    chips = n // 2
    depth = chips // 2
    per = positions // 2
    blocks = cols // LANES
    phases = len(CUTS)
    shown = [0] + [e - 1 for e in CUTS[:-1]] + [CUTS[-1]]
    widths = [(b - a) * LANES for a, b in zip(shown, shown[1:])]
    hbm = pl.BlockSpec(memory_space=pltpu.HBM)
    smem = pl.BlockSpec(memory_space=pltpu.SMEM)
    dma = pltpu.SemaphoreType.DMA
    vmem = pltpu.VMEM
    f32 = jnp.float32
    count = positions * dies
    edges = (ITERS, per // 4, 8, cols)
    return pl.pallas_call(
        functools.partial(strip_kernel, n, dies),
        name="strips",
        out_shape=jax.ShapeDtypeStruct((slots, rows, cols), f32),
        in_specs=[smem, smem, smem, smem, hbm, hbm],
        out_specs=hbm,
        scratch_shapes=[
            tuple(vmem((n * slots, RS, LANES), f32) for _ in range(blocks)),
            vmem((2, per // 2, RS, cols), f32),
            vmem((slots, LANES), jnp.int32),
            vmem((n * slots, LANES), jnp.int32),
            vmem((count // LANES, LANES), jnp.int32),
            pltpu.SMEM((count // LANES, LANES), jnp.int32),
            vmem((ITERS, per, RS, cols), f32),
            vmem(edges, f32),
            vmem(edges, f32),
            vmem(edges, f32),
            vmem(edges, f32),
            vmem((4, 24, cols + 2 * LANES), f32),
            tuple(vmem((chips, positions, RS, w), f32) for w in widths),
            tuple(vmem((slots, rows, w), f32) for w in widths),
            dma((blocks, UNITS, chips)),
            dma((blocks, UNITS, chips)),
            dma((blocks, UNITS)),
            dma((blocks,)),
            dma((blocks,)),
            dma((n,)),
            dma((n,)),
            dma,
            dma((phases, chips)),
            dma((phases, chips)),
            dma((phases,)),
            dma((phases,)),
            dma((phases,)),
            dma((phases, ITERS, HALVES, 2)),
            dma((phases, ITERS, HALVES, 2)),
            dma((phases * HALVES, depth)),
            dma((phases * HALVES, depth)),
            dma((phases * HALVES, depth)),
            dma((phases * HALVES, depth)),
            dma((phases * HALVES, depth)),
            dma((phases * HALVES, depth)),
            dma((phases * HALVES, chips)),
            dma((phases * HALVES, chips)),
            dma((phases,)),
            dma((phases,)),
        ],
        compiler_params=pltpu.CompilerParams(
            collective_id=1, has_side_effects=True, vmem_limit_bytes=56 * 1024 * 1024
        ),
    )(present, kernel, slot_pos, slot_die, die_tiles, strength)


def either(mesh, die_tiles, slot_pos, slot_die, present, strength, kernel):
    n = mesh.shape["die"]
    run = strip_shards if fits(mesh, die_tiles.shape, present.shape, strength.shape) else shards
    return run(n, die_tiles, slot_pos, slot_die, present, strength, kernel)


def solution(mesh):
    placed = (
        P(("wafer", "die"), None, None),
        P(("wafer", "die")),
        P(("wafer", "die")),
        P("wafer", None),
        P("die", None, None),
        P(),
    )
    return jax.shard_map(
        functools.partial(either, mesh),
        mesh=mesh,
        in_specs=placed,
        out_specs=P(("wafer", "die"), None, None),
        check_vma=False,
    )
```

```python
import functools

import jax
import jax.numpy as jnp
from jax import lax
from jax.experimental import pallas as pl
from jax.experimental.pallas import tpu as pltpu
from jax.sharding import PartitionSpec as P

ITERS = 3
RS = 8
LANES = 128
PARTS = 4
HALVES = 2
PER_STEP = 2


def strip_of(q, strips):
    odd = q % 2
    half = q // 2
    return half * (1 - odd) + (strips - 1 - half) * odd


def chip_of(s, strips):
    high = s // (strips // 2)
    return 2 * s * (1 - high) + (2 * (strips - 1 - s) + 1) * high


def greet(n):
    me = lax.axis_index("die")
    barrier = pltpu.get_barrier_semaphore()
    for k in range(1, n):
        pl.semaphore_signal(barrier, inc=1, device_id={"die": (me + k) % n}, device_id_type=pl.DeviceIdType.MESH)
    pl.semaphore_wait(barrier, n - 1)


def remote(src, dst, send, recv, device):
    return pltpu.make_async_remote_copy(
        src_ref=src, dst_ref=dst, send_sem=send, recv_sem=recv,
        device_id={"die": device}, device_id_type=pl.DeviceIdType.MESH,
    )


def refer_kernel(
    n, strips, blocks, cs, dies, positions,
    live, kern, pair, tiles, power, out,
    stacks, strength, pairs, table, where, mean,
    top, bottom, rows_up, rows_down, side_left, side_right, corners, ext, refer,
    send, recv, psend, precv, qsend, qrecv, local, hsend, hrecv, rsend, rrecv, ssend, srecv, own,
):
    me = lax.axis_index("die")
    slots = tiles.shape[0]
    held = power.shape[0]
    chunks = cs // LANES
    s = strip_of(me // blocks, strips)
    c = me % blocks
    groups = positions // 4

    def device(ds, dc):
        return chip_of((s + ds + strips) % strips, strips) * blocks + (c + dc + blocks) % blocks

    def rows_of(peer):
        return pl.ds(pl.multiple_of(strip_of(peer // blocks, strips) * RS, RS), RS)

    def cols_of(peer, start, size):
        return pl.ds(pl.multiple_of((peer % blocks) * cs + start, LANES), size)

    tile_rows = pl.ds(me * slots, slots)
    power_rows = pl.ds(me * held, held)
    greet(n)
    pair_copies = [pltpu.make_async_copy(pair, pairs.at[tile_rows], local.at[0])]
    for k in range(1, n):
        pair_copies.append(remote(pair, pairs.at[tile_rows], qsend.at[k], qrecv.at[k], (me + k) % n))
    for copy in pair_copies:
        copy.start()
    tile_copies = []
    for u in range(chunks):
        wave = [
            pltpu.make_async_copy(
                tiles.at[:, rows_of(me), cols_of(me, u * LANES, LANES)], stacks[u].at[tile_rows], local.at[2 + u]
            )
        ]
        for k in range(1, n):
            peer = (me + k) % n
            wave.append(
                remote(
                    tiles.at[:, rows_of(peer), cols_of(peer, u * LANES, LANES)], stacks[u].at[tile_rows],
                    send.at[u, k], recv.at[u, k], peer,
                )
            )
        for copy in wave:
            copy.start()
        tile_copies.append(wave)
    power_copies = [
        pltpu.make_async_copy(power.at[:, rows_of(me), cols_of(me, 0, cs)], strength.at[power_rows], local.at[1])
    ]
    for k in range(1, n):
        peer = (me + k) % n
        power_copies.append(
            remote(
                power.at[:, rows_of(peer), cols_of(peer, 0, cs)], strength.at[power_rows],
                psend.at[k], precv.at[k], peer,
            )
        )
    for copy in power_copies:
        copy.start()

    for copy in pair_copies:
        copy.wait()
    order = lax.broadcasted_iota(jnp.int32, (n * slots, LANES), 0)
    target = lax.broadcasted_iota(jnp.int32, (n * slots, LANES), 1)
    for w in range(table.shape[0]):
        hit = pairs[...] == target + w * LANES
        table[w : w + 1, :] = jnp.max(jnp.where(hit, order, 0), axis=0, keepdims=True)
    fetch = pltpu.make_async_copy(table, where, local.at[2 + chunks])
    fetch.start()
    fetch.wait()

    def value_of(p, d, some):
        q = p * dies + d
        entry = where[q // LANES, q % LANES]
        if len(some) == 1:
            return stacks[some[0]][entry]
        return jnp.concatenate([stacks[u][entry] for u in some], axis=1)

    first = pl.ds(0, LANES)
    last = pl.ds(cs - LANES, LANES)
    taps = [[kern[5 * a + b] for b in range(5)] for a in range(5)]
    total = taps[0][0]
    for a in range(5):
        for b in range(5):
            if a or b:
                total = total + taps[a][b]

    def exchange(k, h):
        size = groups // HALVES
        g = pl.ds(h * size, size)
        p = pl.ds(h * size * 4, size * 4)
        moves = [
            (bottom.at[k, g], rows_up.at[k, g], 1, 0),
            (top.at[k, g], rows_down.at[k, g], -1, 0),
            (mean.at[k, p, :, last], side_left.at[k, p], 0, 1),
            (mean.at[k, p, :, first], side_right.at[k, p], 0, -1),
            (bottom.at[k, g, :, last], corners.at[k, 0, g], 1, 1),
            (bottom.at[k, g, :, first], corners.at[k, 1, g], 1, -1),
            (top.at[k, g, :, last], corners.at[k, 2, g], -1, 1),
            (top.at[k, g, :, first], corners.at[k, 3, g], -1, -1),
        ]
        copies = [
            remote(src, dst, hsend.at[k, h, m], hrecv.at[k, h, m], device(ds, dc))
            for m, (src, dst, ds, dc) in enumerate(moves)
        ]
        for copy in copies:
            copy.start()
        return copies

    def guard(flag, x):
        return jnp.where(flag, x, jnp.zeros_like(x))

    has_up, has_down, has_left, has_right = s > 0, s < strips - 1, c > 0, c < blocks - 1
    body = pl.ds(LANES, cs)
    right = pl.ds(LANES + cs, LANES)

    def smooth(k, g, j):
        p = 4 * g + j
        pair = pl.ds(2 * j, 2)
        field = mean[k, p]
        ext[j, 6:8, first] = guard(has_up & has_left, corners[k, 0, g, pair, :])
        ext[j, 6:8, body] = guard(has_up, rows_up[k, g, pair, :])
        ext[j, 6:8, right] = guard(has_up & has_right, corners[k, 1, g, pair, :])
        ext[j, 8:16, first] = guard(has_left, side_left[k, p])
        ext[j, 8:16, body] = field
        ext[j, 8:16, right] = guard(has_right, side_right[k, p])
        ext[j, 16:18, first] = guard(has_down & has_left, corners[k, 2, g, pair, :])
        ext[j, 16:18, body] = guard(has_down, rows_down[k, g, pair, :])
        ext[j, 16:18, right] = guard(has_down & has_right, corners[k, 3, g, pair, :])
        shifted = [ext[j, 6 + a : 14 + a, :] for a in range(5)]
        width = cs + 2 * LANES
        acc = None
        for b in range(5):
            part = shifted[0] * taps[0][b]
            for a in range(1, 5):
                part = part + shifted[a] * taps[a][b]
            if b != 2:
                part = pltpu.roll(part, (2 - b) % width, 1)
            part = part[:, LANES : LANES + cs]
            acc = part if acc is None else acc + part
        power_p = strength[p]
        return (field + power_p * acc) / (1.0 + power_p * total)

    def huber(k, g, j, ref, some):
        lanes = pl.ds(some[0] * LANES, len(some) * LANES)
        p = 4 * g + j
        num = None
        for d in range(dies):
            value = value_of(p, d, some)
            weight = live[p * dies + d] / jnp.maximum(jnp.abs(value - ref), 1.5)
            num, den = (weight * value, weight) if num is None else (num + weight * value, den + weight)
        field = num / den
        mean[k, p, :, lanes] = field
        top[k, g, 2 * j : 2 * j + 2, lanes] = field[0:2]
        bottom[k, g, 2 * j : 2 * j + 2, lanes] = field[RS - 2 : RS]

    for u in range(chunks):
        some = (u,)
        for copy in tile_copies[u]:
            copy.wait()

        @pl.loop(0, groups)
        def _(g):
            for j in range(4):
                p = 4 * g + j
                count = live[p * dies]
                num = count * value_of(p, 0, some)
                for d in range(1, dies):
                    share = live[p * dies + d]
                    count = count + share
                    num = num + share * value_of(p, d, some)
                huber(0, g, j, num / jnp.full(num.shape, count), some)

    halo = [exchange(0, h) for h in range(HALVES)]
    for copy in power_copies:
        copy.wait()
    for k in range(1, ITERS):
        later = []
        for h in range(HALVES):
            for copy in halo[h]:
                copy.wait()

            @pl.loop(h * groups // HALVES, (h + 1) * groups // HALVES)
            def _(g):
                for j in range(4):
                    huber(k, g, j, smooth(k - 1, g, j), tuple(range(chunks)))

            later.append(exchange(k, h))
        halo = later

    turn = 1 - 2 * (c % 2)
    ahead = device(turn, 0)
    parts = rsend.shape[1]
    span = positions // parts
    pending = []
    rings = {}
    mine = []

    def forward(t, h):
        strip = (s - turn * t + strips) % strips
        part = pl.ds(h * span, span)
        target = out.at[strip, c, part]
        block = target if t else refer.at[part]
        if t:
            rings[t - 1, h].wait_recv()
        copies = [remote(block, target, ssend.at[t, h, b], srecv.at[t, h, b], device(0, b)) for b in range(1, blocks)]
        if t < strips - 1:
            rings[t, h] = remote(block, target, rsend.at[t, h], rrecv.at[t, h], ahead)
            copies.insert(0, rings[t, h])
        for copy in copies:
            copy.start()
        pending.extend(copies)

    for h in range(parts):
        if h * HALVES % parts == 0:
            for copy in halo[h * HALVES // parts]:
                copy.wait()

        @pl.loop(h * span // 4, (h + 1) * span // 4)
        def _(g):
            for j in range(4):
                refer[4 * g + j] = smooth(ITERS - 1, g, j)

        part = pl.ds(h * span, span)
        mine.append(pltpu.make_async_copy(refer.at[part], out.at[s, c, part], own.at[h]))
        mine[-1].start()
        forward(0, h)
    for t in range(1, strips):
        for h in range(parts):
            forward(t, h)
    for copy in pending:
        copy.wait_send()
    for t in range(strips):
        for h in range(parts):
            for b in range(1, blocks):
                source = (c - b + blocks) % blocks
                strip = (s - (1 - 2 * (source % 2)) * t + strips) % strips
                target = out.at[strip, source, pl.ds(h * span, span)]
                remote(target, target, ssend.at[t, h, b], srecv.at[t, h, b], device(0, b)).wait_recv()
    for copy in mine:
        copy.wait()


def residual_kernel(strips, blocks, cs, pos, die, present, tile, *rest):
    out = rest[-1]
    for u in range(PER_STEP):
        slot = pl.program_id(0) * PER_STEP + u
        keep = present[die[slot], pos[slot]].astype(jnp.float32)
        for s in range(strips):
            for c in range(blocks):
                rows, cols = pl.ds(s * RS, RS), pl.ds(c * cs, cs)
                out[u, rows, cols] = keep * (tile[u, rows, cols] - rest[u][s, c, 0])


def refer_spec(strips, blocks, cs, u):
    return pl.BlockSpec((strips, blocks, 1, RS, cs), lambda i, pos, *_: (0, 0, pos[i * PER_STEP + u], 0, 0))


def shards(n, die_tiles, slot_pos, slot_die, present, strength, kernel):
    slots, rows, cols = die_tiles.shape
    dies, positions = present.shape
    strips = rows // RS
    blocks = n // strips
    cs = cols // blocks
    hbm = pl.BlockSpec(memory_space=pltpu.HBM)
    smem = pl.BlockSpec(memory_space=pltpu.SMEM)
    dma = pltpu.SemaphoreType.DMA
    f32 = jnp.float32

    count = positions * dies
    chunks = cs // LANES
    pair = jnp.broadcast_to((slot_pos * dies + slot_die)[:, None], (slots, LANES))
    groups = positions // 4
    vmem = pltpu.VMEM
    refer = pl.pallas_call(
        functools.partial(refer_kernel, n, strips, blocks, cs, dies, positions),
        name="refer",
        out_shape=jax.ShapeDtypeStruct((strips, blocks, positions, RS, cs), f32),
        in_specs=[smem, smem, pl.BlockSpec(memory_space=pltpu.VMEM), hbm, hbm],
        out_specs=hbm,
        scratch_shapes=[
            tuple(vmem((n * slots, RS, LANES), f32) for _ in range(chunks)),
            vmem((positions, RS, cs), f32),
            vmem((n * slots, LANES), jnp.int32),
            vmem((count // LANES, LANES), jnp.int32),
            pltpu.SMEM((count // LANES, LANES), jnp.int32),
            vmem((ITERS, positions, RS, cs), f32),
            vmem((ITERS, groups, 8, cs), f32),
            vmem((ITERS, groups, 8, cs), f32),
            vmem((ITERS, groups, 8, cs), f32),
            vmem((ITERS, groups, 8, cs), f32),
            vmem((ITERS, positions, RS, LANES), f32),
            vmem((ITERS, positions, RS, LANES), f32),
            vmem((ITERS, 4, groups, 8, LANES), f32),
            vmem((4, 24, cs + 2 * LANES), f32),
            vmem((positions, RS, cs), f32),
            dma((chunks, n)),
            dma((chunks, n)),
            dma((n,)),
            dma((n,)),
            dma((n,)),
            dma((n,)),
            dma((3 + chunks,)),
            dma((ITERS, HALVES, 8)),
            dma((ITERS, HALVES, 8)),
            dma((strips, PARTS)),
            dma((strips, PARTS)),
            dma((strips, PARTS, blocks)),
            dma((strips, PARTS, blocks)),
            dma((PARTS,)),
        ],
        compiler_params=pltpu.CompilerParams(
            collective_id=0, has_side_effects=True, vmem_limit_bytes=56 * 1024 * 1024
        ),
    )(
        present.T.astype(f32).reshape(count),
        kernel.reshape(25),
        pair,
        die_tiles,
        strength,
    )

    return pl.pallas_call(
        functools.partial(residual_kernel, strips, blocks, cs),
        name="residual",
        out_shape=jax.ShapeDtypeStruct((slots, rows, cols), f32),
        grid_spec=pltpu.PrefetchScalarGridSpec(
            num_scalar_prefetch=3,
            grid=(slots // PER_STEP,),
            in_specs=[
                pl.BlockSpec((PER_STEP, rows, cols), lambda i, *_: (i, 0, 0)),
                *[refer_spec(strips, blocks, cs, u) for u in range(PER_STEP)],
            ],
            out_specs=pl.BlockSpec((PER_STEP, rows, cols), lambda i, *_: (i, 0, 0)),
        ),
        compiler_params=pltpu.CompilerParams(vmem_limit_bytes=56 * 1024 * 1024),
    )(slot_pos, slot_die, present, die_tiles, *[refer] * PER_STEP)


CUTS = (5, 8)
AHEAD = 6
BESIDE = 3
UNITS = 2
MESH_ID = pl.DeviceIdType.MESH


def fits(mesh, die_tiles, present, strength):
    n = mesh.shape["die"]
    slots, rows, cols = die_tiles
    dies, positions = present
    return (
        mesh.shape["wafer"] == 2
        and n == 2 * (rows // RS)
        and rows // RS % 4 == 0
        and cols == CUTS[-1] * LANES
        and strength[0] == 2
        and positions == n * 2
        and positions % 16 == 0
        and positions * dies % LANES == 0
    )


def strip_kernel(
    n, dies, present, kern, slot_pos, slot_die, tiles, power, out,
    stacks, strength, pair, pairs, table, where, mean, top, bottom, above, below, ext, refers, windows,
    fsend, frecv, flocal, rsend, rrecv, qsend, qrecv, qlocal, tsend, trecv, tlocal, xsend, xrecv,
    hsend, hrecv, usend, urecv, dsend, drecv, ysend, yrecv, csend, crecv, wload, wstore,
):
    me = lax.axis_index("die")
    wafer = lax.axis_index("wafer")
    chips = n // 2
    depth = chips // 2
    q, c = me // 2, me % 2
    z, y = q // 2, q % 2
    slots, rows, cols = tiles.shape
    per = strength.shape[0] * strength.shape[1]
    groups = per // 4
    blocks = len(stacks)
    phases = len(CUTS)
    ends = CUTS
    starts = (0,) + CUTS[:-1]
    shown = tuple(e - 1 for e in CUTS[:-1]) + (CUTS[-1],)
    hidden = (0,) + shown[:-1]

    def strip_at(zz, yy):
        return 2 * zz + yy * (1 - zz % 2) + (1 - yy) * (zz % 2)

    def chip_at(s):
        zz, odd = s // 2, s % 2
        return 2 * zz + odd * (1 - zz % 2) + (1 - odd) * (zz % 2)

    def lanes(a, b):
        return pl.ds(a * LANES, (b - a) * LANES)

    def rows_of(chip):
        return pl.ds(pl.multiple_of(strip_at(chip // 2, chip % 2) * RS, RS), RS)

    s = strip_at(z, y)
    other = 2 * q + 1 - c

    barrier = pltpu.get_barrier_semaphore()
    for k in range(1, n):
        pl.semaphore_signal(barrier, inc=1, device_id={"die": (me + k) % n}, device_id_type=MESH_ID)
    pl.semaphore_signal(barrier, inc=1, device_id={"wafer": 1 - wafer}, device_id_type=MESH_ID)
    for i in range(slots):
        pair[i : i + 1, :] = jnp.full((1, LANES), slot_pos[i] * dies + slot_die[i], jnp.int32)
    pl.semaphore_wait(barrier, n)

    ours = pl.ds((c * chips + q) * slots, slots)
    pair_copies = [pltpu.make_async_copy(pair, pairs.at[ours], qlocal)]
    for k in range(1, n):
        pair_copies.append(remote(pair, pairs.at[ours], qsend.at[k], qrecv.at[k], (me + k) % n))
    for copy in pair_copies:
        copy.start()

    few = slots // UNITS
    waves = []
    for b in range(blocks):
        for e in range(UNITS):
            some = pl.ds(e * few, few)
            rows_in = pl.ds((c * chips + q) * slots + e * few, few)
            here = pltpu.make_async_copy(
                tiles.at[some, rows_of(q), lanes(b, b + 1)], stacks[b].at[rows_in], flocal.at[b, e]
            )
            there = []
            for k in range(1, chips):
                chip = (q + k) % chips
                there.append(
                    remote(
                        tiles.at[some, rows_of(chip), lanes(b, b + 1)], stacks[b].at[rows_in],
                        fsend.at[b, e, k], frecv.at[b, e, k], 2 * chip + c,
                    )
                )
            waves.append((here, there))
    issued = []

    def pump(last, limit):
        while len(issued) <= min(last, limit - 1, len(waves) - 1):
            here, there = waves[len(issued)]
            issued.append(True)
            here.start()
            for copy in there:
                copy.start()

    half = pl.ds(c * chips * slots, chips * slots)
    relays = [remote(stacks[b].at[half], stacks[b].at[half], rsend.at[b], rrecv.at[b], other) for b in range(blocks)]

    plane, turn = me // chips, me % chips

    def power_copy(u, k):
        chip = (q + k) % chips
        src = power.at[wafer, rows_of(chip), lanes(starts[u], ends[u])]
        dst = strength.at[wafer, turn, :, lanes(starts[u], ends[u])]
        return src, dst, 2 * chip + plane

    def power_remote(u, k):
        src, dst, device = power_copy(u, k)
        return remote(src, dst, tsend.at[u, k], trecv.at[u, turn], device)

    def power_local(u):
        src, dst, _ = power_copy(u, 0)
        return pltpu.make_async_copy(src, dst, tlocal.at[u])

    def power_start(u):
        @pl.when(plane == c)
        def _():
            power_local(u).start()

        @pl.when(plane != c)
        def _():
            power_remote(u, 0).start()

        for k in range(1, chips):
            power_remote(u, k).start()

    def power_cross(u):
        part = strength.at[wafer, :, :, lanes(starts[u], ends[u])]
        return pltpu.make_async_remote_copy(
            src_ref=part, dst_ref=part, send_sem=xsend.at[u], recv_sem=xrecv.at[u],
            device_id={"wafer": 1 - wafer}, device_id_type=MESH_ID,
        )

    def power_pass(u):
        for t in range(chips):
            mine = c * chips + t == me

            @pl.when(mine)
            def _():
                power_local(u).wait()

            @pl.when(jnp.logical_not(mine))
            def _():
                part = strength.at[wafer, t, :, lanes(starts[u], ends[u])]
                remote(part, part, tsend.at[u, 0], trecv.at[u, t], other).wait_recv()

        power_cross(u).start()

    def power_end(u):
        power_cross(u).wait_send()
        part = strength.at[1 - wafer, :, :, lanes(starts[u], ends[u])]
        pltpu.make_async_remote_copy(
            src_ref=part, dst_ref=part, send_sem=xsend.at[u], recv_sem=xrecv.at[u],
            device_id={"wafer": 1 - wafer}, device_id_type=MESH_ID,
        ).wait_recv()

    def power_sent(u):
        @pl.when(plane != c)
        def _():
            power_remote(u, 0).wait_send()

        for k in range(1, chips):
            power_remote(u, k).wait_send()

    pump(UNITS - 1, len(waves))
    power_start(0)
    pump(AHEAD - 1, len(waves))

    loads = [
        pltpu.make_async_copy(tiles.at[:, :, lanes(hidden[u], shown[u])], windows[u], wload.at[u]) for u in range(phases)
    ]
    stores = [
        pltpu.make_async_copy(windows[u], out.at[:, :, lanes(hidden[u], shown[u])], wstore.at[u]) for u in range(phases)
    ]

    taps = [[kern[a, b] for b in range(5)] for a in range(5)]
    total = taps[0][0]
    for a in range(5):
        for b in range(5):
            if a or b:
                total = total + taps[a][b]

    def live(p, d):
        return present[d, p].astype(jnp.float32)

    def value_of(p, d, some):
        at = p * dies + d
        entry = where[at // LANES, at % LANES]
        if len(some) == 1:
            return stacks[some[0]][entry]
        return jnp.concatenate([stacks[b][entry] for b in some], axis=1)

    def huber(k, g, j, ref, some):
        span = lanes(some[0], some[-1] + 1)
        p = per * c + 4 * g + j
        num = None
        for d in range(dies):
            value = value_of(p, d, some)
            weight = live(p, d) / jnp.maximum(jnp.abs(value - ref), 1.5)
            num, den = (weight * value, weight) if num is None else (num + weight * value, den + weight)
        field = num / den
        mean[k, 4 * g + j, :, span] = field
        top[k, g, 2 * j : 2 * j + 2, span] = field[0:2]
        bottom[k, g, 2 * j : 2 * j + 2, span] = field[RS - 2 : RS]

    def guard(flag, x):
        return jnp.where(flag, x, jnp.zeros_like(x))

    has_up, has_down = s > 0, s < chips - 1

    def smooth(k, g, j, some, more):
        first, last = some[0], some[-1] + 1
        low = first - 1 if first else first
        high = last + 1 if more else last
        src = lanes(low, high)
        dst = lanes(low - first + 1, high - first + 1)
        width = (last - first + 2) * LANES
        rows2 = pl.ds(2 * j, 2)
        p = 4 * g + j
        ext[j, 6:8, dst] = guard(has_up, above[k, g, rows2, src])
        ext[j, 8:16, dst] = mean[k, p, :, src]
        ext[j, 16:18, dst] = guard(has_down, below[k, g, rows2, src])
        edge = jnp.zeros((24, LANES), jnp.float32)
        if not first:
            ext[j, :, 0:LANES] = edge
        if not more:
            ext[j, :, width - LANES : width] = edge
        shifted = [ext[j, 6 + a : 14 + a, 0:width] for a in range(5)]
        acc = None
        for b in range(5):
            part = shifted[0] * taps[0][b]
            for a in range(1, 5):
                part = part + shifted[a] * taps[a][b]
            if b != 2:
                part = pltpu.roll(part, (2 - b) % width, 1)
            part = part[:, LANES : width - LANES]
            acc = part if acc is None else acc + part
        field = mean[k, p, :, lanes(first, last)]
        power_p = strength[p % 2, p // 2, :, lanes(first, last)]
        return (field + power_p * acc) / (1.0 + power_p * total)

    def halo(u, k, h, start):
        first = starts[u] if k == 0 else hidden[u]
        span = lanes(first, ends[u])
        size = groups // HALVES
        g = pl.ds(h * size, size)
        down = remote(
            bottom.at[k, g, :, span], above.at[k, g, :, span], hsend.at[u, k, h, 0], hrecv.at[u, k, h, 0],
            2 * chip_at((s + 1) % chips) + c,
        )
        up = remote(
            top.at[k, g, :, span], below.at[k, g, :, span], hsend.at[u, k, h, 1], hrecv.at[u, k, h, 1],
            2 * chip_at((s + chips - 1) % chips) + c,
        )
        if start:

            @pl.when(has_down)
            def _():
                down.start()

            @pl.when(has_up)
            def _():
                up.start()

            return

        @pl.when(has_down)
        def _():
            down.wait_send()
            up.wait_recv()

        @pl.when(has_up)
        def _():
            up.wait_send()
            down.wait_recv()

    def part(v, zz, yy, cc):
        u, h = v // HALVES, v % HALVES
        return refers[u].at[strip_at(zz, yy), pl.ds(cc * per + h * (per // HALVES), per // HALVES)]

    def to_up(u, t):
        block = part(u, (z - t + depth) % depth, y, c)
        return remote(block, block, usend.at[u, t], urecv.at[u, t], (me + 4) % n)

    def to_down(u, t):
        block = part(u, (z + t) % depth, y, c)
        return remote(block, block, dsend.at[u, t], drecv.at[u, t], (me + n - 4) % n)

    def to_side(u, zz):
        block = part(u, zz, y, c)
        return remote(block, block, ysend.at[u, zz], yrecv.at[u, zz], 4 * z + 2 * (1 - y) + c)

    def to_core(u, zz, yy):
        block = part(u, zz, yy, c)
        return remote(block, block, csend.at[u, 2 * zz + yy], crecv.at[u, 2 * zz + yy], other)

    def show(u):
        @pl.when(z < depth - 1)
        def _():
            to_up(u, 0).start()

        @pl.when(z > 0)
        def _():
            to_down(u, 0).start()

        to_side(u, z).start()
        to_core(u, z, y).start()

    def hop(u, t):
        @pl.when(z - t >= 0)
        def _():
            block = part(u, (z - t + depth) % depth, y, c)
            remote(block, block, usend.at[u, t - 1], urecv.at[u, t - 1], other).wait_recv()
            if t < depth - 1:

                @pl.when(z < depth - 1)
                def _():
                    to_up(u, t).start()

            to_side(u, (z - t + depth) % depth).start()
            to_core(u, (z - t + depth) % depth, y).start()

        @pl.when(z + t <= depth - 1)
        def _():
            block = part(u, (z + t) % depth, y, c)
            remote(block, block, dsend.at[u, t - 1], drecv.at[u, t - 1], other).wait_recv()
            if t < depth - 1:

                @pl.when(z > 0)
                def _():
                    to_down(u, t).start()

            to_side(u, (z + t) % depth).start()
            to_core(u, (z + t) % depth, y).start()

    def hops(u, t):
        for v in range(max(u, 0) * HALVES, (u + 1) * HALVES):
            hop(v, t)

    def sides(u):
        for t in range(depth):
            zz = (z + t) % depth
            block = part(u, zz, 1 - y, c)
            remote(block, block, ysend.at[u, zz], yrecv.at[u, zz], other).wait_recv()
            to_core(u, zz, 1 - y).start()

    def residual(u):
        for v in range(u * HALVES, (u + 1) * HALVES):
            for q2 in range(chips):
                block = part(v, q2 // 2, q2 % 2, 1 - c)
                remote(block, block, csend.at[v, q2], crecv.at[v, q2], other).wait_recv()
        loads[u].wait()

        @pl.loop(0, slots)
        def _(i):
            at = slot_pos[i]
            keep = present[slot_die[i], at].astype(jnp.float32)
            for strip in range(chips):
                span = pl.ds(strip * RS, RS)
                windows[u][i, span, :] = keep * (windows[u][i, span, :] - refers[u][strip, at])

        stores[u].start()

    def sent(u):
        for t in range(depth - 1):

            @pl.when((z < depth - 1) & (z - t >= 0))
            def _():
                to_up(u, t).wait_send()

            @pl.when((z > 0) & (z + t <= depth - 1))
            def _():
                to_down(u, t).wait_send()

        for zz in range(depth):
            to_side(u, zz).wait_send()
            for yy in range(2):
                to_core(u, zz, yy).wait_send()

    size = groups // HALVES
    for u in range(phases):
        fresh = tuple(range(starts[u], ends[u]))
        again = tuple(range(hidden[u], ends[u]))
        done = tuple(range(hidden[u], shown[u]))
        loads[u].start()
        for b in fresh:
            for e in range(b * UNITS, (b + 1) * UNITS):
                here, there = waves[e]
                here.wait()
                for copy in there:
                    copy.wait_recv()
                pump(e + AHEAD, ends[u] * UNITS + BESIDE)
            relays[b].start()
            if u + 1 < phases and b == fresh[0]:
                power_start(u + 1)
        if u == 0:
            for copy in pair_copies:
                copy.wait()
            order = lax.broadcasted_iota(jnp.int32, (n * slots, LANES), 0)
            target = lax.broadcasted_iota(jnp.int32, (n * slots, LANES), 1)
            for w in range(table.shape[0]):
                hit = pairs[...] == target + w * LANES
                table[w : w + 1, :] = jnp.max(jnp.where(hit, order, 0), axis=0, keepdims=True)
            fetch = pltpu.make_async_copy(table, where, qlocal)
            fetch.start()
            fetch.wait()
        power_pass(u)
        for b in fresh:
            part_b = stacks[b].at[pl.ds((1 - c) * chips * slots, chips * slots)]
            remote(part_b, part_b, rsend.at[b], rrecv.at[b], other).wait_recv()

        for h in range(HALVES):

            @pl.loop(h * size, (h + 1) * size)
            def _(g):
                for j in range(4):
                    p = per * c + 4 * g + j
                    count = live(p, 0)
                    num = count * value_of(p, 0, fresh)
                    for d in range(1, dies):
                        share = live(p, d)
                        count = count + share
                        num = num + share * value_of(p, d, fresh)
                    huber(0, g, j, num / jnp.full(num.shape, count), fresh)

            halo(u, 0, h, True)
        power_end(u)
        hops(u - 1, 1)
        if u > 1:
            for v in range((u - 2) * HALVES, (u - 1) * HALVES):
                sides(v)
        for k in range(1, ITERS):
            for h in range(HALVES):
                halo(u, k - 1, h, False)
                pump(len(waves), len(issued) + 1)

                @pl.loop(h * size, (h + 1) * size)
                def _(g):
                    for j in range(4):
                        huber(k, g, j, smooth(k - 1, g, j, again, False), again)

                halo(u, k, h, True)
            hops(u - 1, k + 1)
            if u > 1 and k == 1:
                residual(u - 2)
        for h in range(HALVES):
            halo(u, ITERS - 1, h, False)

            @pl.loop(h * size, (h + 1) * size)
            def _(g):
                for j in range(4):
                    value = smooth(ITERS - 1, g, j, done, done[-1] + 1 < ends[u])
                    refers[u][s, per * c + 4 * g + j] = value

            show(u * HALVES + h)
        pump(len(waves), len(issued) + 1)
    u = phases - 1
    hops(u, 1)
    hops(u, 2)
    for v in range((u - 1) * HALVES, u * HALVES):
        sides(v)
    hops(u, 3)
    residual(u - 1)
    for v in range(u * HALVES, (u + 1) * HALVES):
        sides(v)
    residual(u)
    for here, there in waves:
        for copy in there:
            copy.wait_send()
    for copy in relays:
        copy.wait_send()
    for u in range(phases):
        power_sent(u)
        for v in range(u * HALVES, (u + 1) * HALVES):
            sent(v)
        stores[u].wait()


def strip_shards(n, die_tiles, slot_pos, slot_die, present, strength, kernel):
    slots, rows, cols = die_tiles.shape
    dies, positions = present.shape
    chips = n // 2
    depth = chips // 2
    per = positions // 2
    blocks = cols // LANES
    phases = len(CUTS)
    shown = [0] + [e - 1 for e in CUTS[:-1]] + [CUTS[-1]]
    widths = [(b - a) * LANES for a, b in zip(shown, shown[1:])]
    hbm = pl.BlockSpec(memory_space=pltpu.HBM)
    smem = pl.BlockSpec(memory_space=pltpu.SMEM)
    dma = pltpu.SemaphoreType.DMA
    vmem = pltpu.VMEM
    f32 = jnp.float32
    count = positions * dies
    edges = (ITERS, per // 4, 8, cols)
    return pl.pallas_call(
        functools.partial(strip_kernel, n, dies),
        name="strips",
        out_shape=jax.ShapeDtypeStruct((slots, rows, cols), f32),
        in_specs=[smem, smem, smem, smem, hbm, hbm],
        out_specs=hbm,
        scratch_shapes=[
            tuple(vmem((n * slots, RS, LANES), f32) for _ in range(blocks)),
            vmem((2, per // 2, RS, cols), f32),
            vmem((slots, LANES), jnp.int32),
            vmem((n * slots, LANES), jnp.int32),
            vmem((count // LANES, LANES), jnp.int32),
            pltpu.SMEM((count // LANES, LANES), jnp.int32),
            vmem((ITERS, per, RS, cols), f32),
            vmem(edges, f32),
            vmem(edges, f32),
            vmem(edges, f32),
            vmem(edges, f32),
            vmem((4, 24, cols + 2 * LANES), f32),
            tuple(vmem((chips, positions, RS, w), f32) for w in widths),
            tuple(vmem((slots, rows, w), f32) for w in widths),
            dma((blocks, UNITS, chips)),
            dma((blocks, UNITS, chips)),
            dma((blocks, UNITS)),
            dma((blocks,)),
            dma((blocks,)),
            dma((n,)),
            dma((n,)),
            dma,
            dma((phases, chips)),
            dma((phases, chips)),
            dma((phases,)),
            dma((phases,)),
            dma((phases,)),
            dma((phases, ITERS, HALVES, 2)),
            dma((phases, ITERS, HALVES, 2)),
            dma((phases * HALVES, depth)),
            dma((phases * HALVES, depth)),
            dma((phases * HALVES, depth)),
            dma((phases * HALVES, depth)),
            dma((phases * HALVES, depth)),
            dma((phases * HALVES, depth)),
            dma((phases * HALVES, chips)),
            dma((phases * HALVES, chips)),
            dma((phases,)),
            dma((phases,)),
        ],
        compiler_params=pltpu.CompilerParams(
            collective_id=1, has_side_effects=True, vmem_limit_bytes=56 * 1024 * 1024
        ),
    )(present, kernel, slot_pos, slot_die, die_tiles, strength)


def either(mesh, die_tiles, slot_pos, slot_die, present, strength, kernel):
    n = mesh.shape["die"]
    run = strip_shards if fits(mesh, die_tiles.shape, present.shape, strength.shape) else shards
    return run(n, die_tiles, slot_pos, slot_die, present, strength, kernel)


def solution(mesh):
    placed = (
        P(("wafer", "die"), None, None),
        P(("wafer", "die")),
        P(("wafer", "die")),
        P("wafer", None),
        P("die", None, None),
        P(),
    )
    return jax.shard_map(
        functools.partial(either, mesh),
        mesh=mesh,
        in_specs=placed,
        out_specs=P(("wafer", "die"), None, None),
        check_vma=False,
    )
```
